32 devices in a mesh: band: 16 (over z, y, x), dp: 2 (over core).
Axes of the slice: x: 2, y: 2, z: 4, core: 2. Of those that a mesh axis runs over, the one named last changes fastest.
Arguments:
- pages: bfloat16 [32768, 256], P('band', 'dp'), may hold values from -6 to 6
- band_tiles: bfloat16 [256, 3, 128, 128], P('band'), may hold values from 0 to 1, as said below
- off_tiles: bfloat16 [256, 128, 128], P('band'), may hold values from 0 to 1, as said below
- off_row: int32 [256], P('band'), may hold values from 0 to 15
- requests: int32 [256], P('band'), may hold values from 0 to 15
- label_page: int32 [16384], P('band'), may hold values from 0 to 2047
- labels: int32 [16384], P(('band', 'dp')), may hold values from 0 to 255
- w_first: bfloat16 [768, 1024], replicated, may hold values from -0.21875 to 0.21875
- w_second: bfloat16 [1024, 256], replicated
Outputs:
- prop_a: bfloat16 [32768, 256], P('band', 'dp')
- prop_t: bfloat16 [32768, 256], P('band', 'dp')
- prop_aat: bfloat16 [32768, 256], P('band', 'dp')
- grad_w1: bfloat16 [768, 1024], replicated
- grad_w2: bfloat16 [1024, 256], replicated
The draws below stay inside these ranges and needn't reach their ends.
Inputs may be any that keep to these rules, and one draw needn't show every extreme that they name: `off_row`: row block within a band. `requests`: row block within a band. `band_tiles`: links weighted between 0 and 1, about half of the entries zero. `off_tiles`: links weighted between 0 and 1, about half of the entries zero.
All inputs are finite; a program needn't handle non-finite values.
Results may differ from the reference program's by a relative error of at most 0.011.
Values may be sent and summed in bfloat16 or wider, within the bound.
A program may use at most 128 MiB of HBM per device.

```python
import math
import jax
import jax.numpy as jnp
from jax import lax

F = 256
HID = 1024
CLASSES = 256
TILE = 128
P_DEV = 2048
LAB_DEV = 1024
IN_F = 768
NB = 16
PAGES = 32768
BLOCKS = 256
OFFS = 256
LABELS = 16384
N_BAND = 16


def link_weights(key, shape):
    key_mask = jax.random.fold_in(key, 11)
    key_value = jax.random.fold_in(key, 12)
    present = jax.random.bernoulli(key_mask, 0.5, shape).astype(jnp.float32)
    values = jnp.exp(jax.random.uniform(key_value, shape, jnp.float32, math.log(0.02), math.log(0.12)))
    return present * values


def draw_band_tiles(key, part):
    return link_weights(key, (BLOCKS, 3, TILE, TILE)).astype(jnp.bfloat16)


def draw_off_tiles(key, part):
    return link_weights(key, (OFFS, TILE, TILE)).astype(jnp.bfloat16)


def draw_w_second(key, part):
    key_base = jax.random.fold_in(key, 21)
    values = jnp.clip(jax.random.normal(key_base, (HID, CLASSES), jnp.float32), -6.0, 6.0) * HID ** (-0.5)
    return values.astype(jnp.bfloat16)


def touch_ends(drawn, stream_key, smallest, largest):
    longest = drawn.shape.index(max(drawn.shape))
    spots = []
    for shift in (0, 1):
        where = [jax.random.randint(jax.random.fold_in(stream_key, axis), (), 0, length) for axis, length in enumerate(drawn.shape)]
        where[longest] = (where[longest] + shift) % drawn.shape[longest]
        spots.append(tuple(where))
    return drawn.at[spots[0]].set(smallest).at[spots[1]].set(largest)


def block_scale(stream_key, extent, pieces, least, top_value):
    factor_of, own = 1.0, jax.random.fold_in(stream_key, 6)
    for position, shards_of in pieces:
        draws = jnp.exp(jax.random.uniform(jax.random.fold_in(own, position), (shards_of,), jnp.float32, least / len(pieces), top_value / len(pieces)))
        factor_of = factor_of * jnp.repeat(draws, extent[position] // shards_of).reshape([-1 if axis == position else 1 for axis in range(len(extent))])
    return factor_of


def gaussian(own_key, extent, width, most, cuts=(), held_as=jnp.bfloat16):
    gain = block_scale(own_key, extent, cuts, -0.22, 0.18) if cuts else 1.0
    array = jax.random.normal(own_key, extent, jnp.float32) * width * gain
    return jnp.minimum(jnp.maximum(array, -most), most).astype(held_as)


def setup_inputs(seed: int = 0) -> dict:
    streams_of = jax.random.split(jax.random.key(seed), 10)
    return {
        "pages": gaussian(streams_of[0], (PAGES, F), 1.0, 6.0, ((0, 16), (1, 2))),
        "band_tiles": draw_band_tiles(jax.random.fold_in(streams_of[9], 71), 0),
        "off_tiles": draw_off_tiles(jax.random.fold_in(streams_of[9], 71), 0),
        "off_row": touch_ends(jax.random.randint(streams_of[3], (OFFS,), 0, NB), jax.random.fold_in(streams_of[3], 1), 0, NB - 1).astype(jnp.int32),
        "requests": touch_ends(jax.random.randint(streams_of[4], (OFFS,), 0, NB), jax.random.fold_in(streams_of[4], 1), 0, NB - 1).astype(jnp.int32),
        "label_page": touch_ends(jax.random.randint(streams_of[5], (LABELS,), 0, P_DEV), jax.random.fold_in(streams_of[5], 1), 0, P_DEV - 1).astype(jnp.int32),
        "labels": touch_ends(jax.random.randint(streams_of[6], (LABELS,), 0, CLASSES), jax.random.fold_in(streams_of[6], 1), 0, CLASSES - 1).astype(jnp.int32),
        "w_first": gaussian(streams_of[7], (IN_F, HID), IN_F ** -0.5, 0.21875),
        "w_second": draw_w_second(jax.random.fold_in(streams_of[9], 71), 0),
    }


def band_forward(band_tiles, field):
    block_count = P_DEV // TILE
    v_blocks = field.reshape(N_BAND * block_count, TILE, F)
    zero_block = jnp.zeros((1, TILE, F), field.dtype)
    padded = jnp.concatenate([zero_block, v_blocks, zero_block], 0)
    band_set = band_tiles.reshape(N_BAND, block_count, 3, TILE, TILE)

    def per_device(device_id):
        window = lax.dynamic_slice_in_dim(padded, device_id * block_count, block_count + 2, 0)
        windows = jnp.stack([window[0:block_count], window[1:block_count + 1], window[2:block_count + 2]], 1)
        tiles_here = lax.dynamic_index_in_dim(band_set, device_id, 0, keepdims=False)
        return jnp.einsum('rjab,rjbf->raf', tiles_here.astype(jnp.float32), windows.astype(jnp.float32),
                          precision=lax.Precision.HIGHEST)

    result = lax.map(per_device, jnp.arange(N_BAND, dtype=jnp.int32))
    return result.reshape(PAGES, F)


def band_adjoint(band_tiles, field):
    block_count = P_DEV // TILE
    v_blocks = field.reshape(N_BAND, block_count, TILE, F)
    band_set = band_tiles.reshape(N_BAND, block_count, 3, TILE, TILE)

    def per_device(pair):
        tiles_here, blocks_here = pair
        adjoint_terms = jnp.einsum('rjab,raf->rjbf', tiles_here.astype(jnp.float32), blocks_here.astype(jnp.float32),
                                   precision=lax.Precision.HIGHEST)
        accumulated = jnp.zeros((block_count + 2, TILE, F), jnp.float32)
        accumulated = accumulated.at[0:block_count].add(adjoint_terms[:, 0])
        accumulated = accumulated.at[1:block_count + 1].add(adjoint_terms[:, 1])
        accumulated = accumulated.at[2:block_count + 2].add(adjoint_terms[:, 2])
        return accumulated

    accumulated = lax.map(per_device, (band_set, v_blocks))
    inner_part = accumulated[:, 1:block_count + 1]
    low_rim = accumulated[:, 0]
    high_rim = accumulated[:, block_count + 1]
    from_right = jnp.concatenate([low_rim[1:], jnp.zeros_like(low_rim[:1])], 0)
    from_left = jnp.concatenate([jnp.zeros_like(high_rim[:1]), high_rim[:-1]], 0)
    inner_part = inner_part.at[:, block_count - 1].add(from_right)
    inner_part = inner_part.at[:, 0].add(from_left)
    return inner_part.reshape(PAGES, F)


def off_forward(off_tiles, off_row, requests, field):
    block_count = P_DEV // TILE
    v_blocks = field.reshape(N_BAND * block_count, TILE, F)
    tile_set = off_tiles.reshape(N_BAND, N_BAND, TILE, TILE)
    row_ids = off_row.reshape(N_BAND, N_BAND)
    request_ids = requests.reshape(N_BAND, N_BAND)
    peer_base = jnp.arange(N_BAND, dtype=jnp.int32) * block_count

    def per_device(triple):
        tiles_here, rows_here, wanted = triple
        columns = (peer_base + wanted).astype(jnp.int32)
        fetched = v_blocks[columns]
        products = jnp.einsum('kab,kbf->kaf', tiles_here.astype(jnp.float32), fetched.astype(jnp.float32),
                              precision=lax.Precision.HIGHEST)
        row_hot = (rows_here[None, :] == jnp.arange(block_count, dtype=jnp.int32)[:, None]).astype(jnp.float32)
        return jnp.einsum('rk,kaf->raf', row_hot, products, precision=lax.Precision.HIGHEST)

    result = lax.map(per_device, (tile_set, row_ids, request_ids))
    return result.reshape(PAGES, F)


def off_adjoint(off_tiles, off_row, requests, field):
    block_count = P_DEV // TILE
    v_blocks = field.reshape(N_BAND * block_count, TILE, F)
    tile_set = off_tiles.reshape(N_BAND, N_BAND, TILE, TILE)
    row_ids = off_row.reshape(N_BAND, N_BAND)
    request_ids = requests.reshape(N_BAND, N_BAND)
    peer_base = jnp.arange(N_BAND, dtype=jnp.int32) * block_count

    def step_fn(total, quad):
        device_id, tiles_here, rows_here, wanted = quad
        sources = v_blocks[(device_id * block_count + rows_here).astype(jnp.int32)]
        term_block = jnp.einsum('kab,kaf->kbf', tiles_here.astype(jnp.float32), sources.astype(jnp.float32),
                                precision=lax.Precision.HIGHEST)
        term_block = lax.optimization_barrier(term_block.astype(jnp.bfloat16)).astype(jnp.float32)
        columns = (peer_base + wanted).astype(jnp.int32)
        return total.at[columns].add(term_block), None

    start = jnp.zeros((N_BAND * block_count, TILE, F), jnp.float32)
    total, _ = lax.scan(step_fn, start, (jnp.arange(N_BAND, dtype=jnp.int32), tile_set, row_ids, request_ids))
    return total.reshape(PAGES, F)


def reference(pages, band_tiles, off_tiles, off_row, requests, label_page, labels, w_first, w_second):
    prop_a = (band_forward(band_tiles, pages) + off_forward(off_tiles, off_row, requests, pages)).astype(jnp.bfloat16)
    prop_t = (band_adjoint(band_tiles, pages) + off_adjoint(off_tiles, off_row, requests, pages)).astype(jnp.bfloat16)
    prop_aat = (band_forward(band_tiles, prop_t) + off_forward(off_tiles, off_row, requests, prop_t)).astype(jnp.bfloat16)
    global_rows = ((jnp.arange(LABELS, dtype=jnp.int32) // LAB_DEV) * P_DEV + label_page).astype(jnp.int32)
    features = jnp.concatenate([prop_a[global_rows], prop_t[global_rows], prop_aat[global_rows]], 1)
    pre_act = jnp.dot(features, w_first, preferred_element_type=jnp.float32)
    sigma = jax.nn.sigmoid(pre_act)
    hidden = (pre_act * sigma).astype(jnp.bfloat16)
    logits = jnp.dot(hidden, w_second, preferred_element_type=jnp.float32)
    probabilities = jax.nn.softmax(logits, axis=-1)
    label_hot = (labels[:, None] == jnp.arange(CLASSES, dtype=jnp.int32)[None, :]).astype(jnp.float32)
    errors = ((probabilities - label_hot) / LAB_DEV).astype(jnp.bfloat16)
    grad_w2 = jnp.dot(hidden.T, errors, preferred_element_type=jnp.float32).astype(jnp.bfloat16)
    slope = sigma * (1.0 + pre_act * (1.0 - sigma))
    back_signal = (jnp.dot(errors, w_second.T, preferred_element_type=jnp.float32) * slope).astype(jnp.bfloat16)
    grad_w1 = jnp.dot(features.T, back_signal, preferred_element_type=jnp.float32).astype(jnp.bfloat16)
    return prop_a, prop_t, prop_aat, grad_w1, grad_w2
```

```python
import functools

import jax
import jax.numpy as jnp
from jax import lax
from jax.experimental import pallas as pl
from jax.experimental.pallas import tpu as pltpu
from jax.sharding import PartitionSpec as P


def padded_2(cells, sides, width):
    for axis, dim in sides:
        count = lax.axis_size(axis)
        ends = count - 1
        head = lax.slice_in_dim(cells, 0, width, axis=dim)
        tail = lax.slice_in_dim(cells, cells.shape[dim] - width, cells.shape[dim], axis=dim)
        cells = jnp.concatenate(
            [
                lax.ppermute(tail, axis, [(i, (i + 1) % count) for i in range(ends)]),
                cells,
                lax.ppermute(head, axis, [((i + 1) % count, i) for i in range(ends)]),
            ],
            axis=dim,
        )
    return cells


MESH = pl.DeviceIdType.MESH


def greet_all(n):
    b, other = lax.axis_index("band"), 1 - lax.axis_index("dp")
    barrier = pltpu.get_barrier_semaphore()
    pl.semaphore_signal(barrier, inc=1, device_id={"dp": other}, device_id_type=MESH)

    def greet(d, _):
        pl.semaphore_signal(
            barrier, inc=1, device_id={"band": lax.rem(b + d, n)}, device_id_type=MESH
        )
        return 0

    lax.fori_loop(1, n, greet, 0)
    pl.semaphore_wait(barrier, n)


def remote(src, dst, send_sem, recv_sem, **where):
    return pltpu.make_async_remote_copy(
        src_ref=src, dst_ref=dst, send_sem=send_sem, recv_sem=recv_sem,
        device_id=where, device_id_type=MESH,
    )


def each(start, stop, body):
    def step(d, _):
        body(d)
        return 0

    lax.fori_loop(start, stop, step, 0)


def reduce_kernel(
    n, cols, g1, g2, out, recv1, recv2, send, land, acc,
    s_core, r_core, s_rs, r_rs, s_ag, r_ag, s_fw, r_fw,
):
    b, h = lax.axis_index("band"), lax.axis_index("dp")
    o = 1 - h
    width = send.shape[2] // cols
    top = recv1.shape[0]
    step_rows = send.shape[1]
    quarter = recv2.shape[0] // 4
    wide = recv2.shape[1]

    def part(c):
        return lax.div(c, cols), pl.ds(pl.multiple_of(lax.rem(c, cols) * width, 128), width)

    greet_all(n)
    first = remote(g1.at[o], recv1, s_core.at[0], r_core.at[0], dp=o)
    second = remote(g2.at[o], recv2, s_core.at[1], r_core.at[1], dp=o)
    first.start()
    second.start()
    first.wait()

    def fill_first(i):
        rows = pl.ds(pl.multiple_of(i * step_rows, step_rows), step_rows)
        send[i] = (g1[h, rows] + recv1[rows]).astype(jnp.bfloat16)

    each(0, top // step_rows, fill_first)
    second.wait()

    def fill_second(i):
        for j in range(4):
            rows = pl.ds(pl.multiple_of(j * quarter + i * step_rows, step_rows), step_rows)
            send[top // step_rows + i, :, j * wide : (j + 1) * wide] = (
                g2[h, rows] + recv2[rows]
            ).astype(jnp.bfloat16)

    each(0, quarter // step_rows, fill_second)

    def scatter(d):
        t = lax.rem(b + d, n)
        i, w = part(t)
        return remote(send.at[i, :, w], land.at[d], s_rs.at[d], r_rs.at[d], band=t)

    each(1, n, lambda d: scatter(d).start())
    mine, mine_w = part(b)
    acc[...] = send[mine, :, mine_w].astype(jnp.float32)

    def collect(d):
        scatter(d).wait_recv()
        acc[...] += land[d].astype(jnp.float32)

    each(1, n, collect)
    out[h, mine, :, mine_w] = acc[...].astype(jnp.bfloat16)

    def spread(d):
        spot = out.at[h, mine, :, mine_w]
        return remote(spot, spot, s_ag.at[d], r_ag.at[d], band=lax.rem(b + d, n))

    def arrival(d):
        i, w = part(lax.rem(b + n - d, n))
        spot = out.at[h, i, :, w]
        return remote(spot, spot, s_ag.at[d], r_ag.at[d], band=lax.rem(b + d, n))

    def forward(d):
        i, w = part(lax.rem(b + n - d, n))
        spot = out.at[h, i, :, w]
        return remote(spot, spot, s_fw.at[d], r_fw.at[d], dp=o)

    def forwarded(d):
        i, w = part(lax.rem(b + n - d, n))
        spot = out.at[o, i, :, w]
        return remote(spot, spot, s_fw.at[d], r_fw.at[d], dp=o)

    each(1, n, lambda d: spread(d).start())
    forward(0).start()

    def pass_on(d):
        arrival(d).wait_recv()
        forward(d).start()

    each(1, n, pass_on)

    def finish(d):
        scatter(d).wait_send()
        spread(d).wait_send()

    each(1, n, finish)

    def finish_pair(d):
        forward(d).wait_send()
        forwarded(d).wait_recv()

    each(0, n, finish_pair)


def summed_gradients(grad_first, grad_second):
    n = lax.axis_size("band")
    cols = max(1, n // 16)
    in_f, hid = grad_first.shape
    classes = grad_second.shape[1]
    half_rows = (grad_first.size + grad_second.size) // (2 * hid)
    step_rows = half_rows * cols // n
    blocks = half_rows // step_rows
    top = in_f // 2
    vmem = pl.BlockSpec(memory_space=pltpu.VMEM)
    dma = pltpu.SemaphoreType.DMA
    packed = pl.pallas_call(
        functools.partial(reduce_kernel, n, cols),
        out_shape=jax.ShapeDtypeStruct((2, blocks, step_rows, hid), jnp.bfloat16),
        in_specs=[vmem] * 2,
        out_specs=vmem,
        scratch_shapes=[
            pltpu.VMEM((top, hid), jnp.float32),
            pltpu.VMEM((hid // 2, classes), jnp.float32),
            pltpu.VMEM((blocks, step_rows, hid), jnp.bfloat16),
            pltpu.VMEM((n, step_rows, hid // cols), jnp.bfloat16),
            pltpu.VMEM((step_rows, hid // cols), jnp.float32),
            dma((2,)), dma((2,)), dma((n,)), dma((n,)), dma((n,)), dma((n,)), dma((n,)), dma((n,)),
        ],
        compiler_params=pltpu.CompilerParams(
            collective_id=0, has_side_effects=True, vmem_limit_bytes=40 * 2**20
        ),
        name="grad_sum",
    )(grad_first.reshape(2, top, hid), grad_second.reshape(2, hid // 2, classes))
    packed = packed.reshape(2, half_rows, hid)
    parts = hid // classes
    low = packed[:, top:].reshape(2, half_rows - top, parts, classes)
    return (
        packed[:, :top].reshape(in_f, hid),
        low.transpose(0, 2, 1, 3).reshape(hid, classes),
    )


def per_device(
    pages, band_tiles, off_tiles, off_row, requests, label_page, labels, w_first, w_second
):
    tile_size = band_tiles.shape[-1]
    rows_dev, feat_half = pages.shape
    block_count = rows_dev // tile_size
    block_iota = jnp.arange(block_count, dtype=jnp.int32)
    served = lax.all_to_all(requests, "band", split_axis=0, concat_axis=0, tiled=True)
    row_hot = (off_row[None, :] == block_iota[:, None]).astype(jnp.float32)
    served_hot = (served[None, :] == block_iota[:, None]).astype(jnp.float32)

    def band_forward(field):
        padded = padded_2(field, (("band", 0),), tile_size)
        blocks = padded.reshape(block_count + 2, tile_size, feat_half)
        windows = jnp.stack(
            [blocks[0:block_count], blocks[1 : block_count + 1], blocks[2 : block_count + 2]], 1
        )
        return jnp.einsum("rjab,rjbf->raf", band_tiles, windows, preferred_element_type=jnp.float32)

    def off_apply(fetched):
        products = jnp.einsum(
            "kab,kbf->kaf", off_tiles, fetched, preferred_element_type=jnp.float32
        )
        return jnp.einsum("rk,kaf->raf", row_hot, products, precision=lax.Precision.HIGHEST)

    def serve_blocks(field):
        return jnp.take(field.reshape(block_count, tile_size, feat_half), served, axis=0)

    own_blocks = pages.reshape(block_count, tile_size, feat_half)
    near_part = band_forward(pages)
    adjoint_terms = jnp.einsum(
        "rjab,raf->rjbf", band_tiles, own_blocks, preferred_element_type=jnp.float32
    )
    accumulated = jnp.zeros((block_count + 2, tile_size, feat_half), jnp.float32)
    accumulated = accumulated.at[0:block_count].add(adjoint_terms[:, 0])
    accumulated = accumulated.at[1 : block_count + 1].add(adjoint_terms[:, 1])
    accumulated = accumulated.at[2 : block_count + 2].add(adjoint_terms[:, 2])
    rim_rows = jnp.concatenate([accumulated[0], accumulated[block_count + 1]], 0)
    received = padded_2(rim_rows, (("band", 0),), tile_size)
    inner_part = accumulated[1 : block_count + 1]
    inner_part = inner_part.at[0].add(received[0:tile_size])
    inner_part = inner_part.at[block_count - 1].add(received[3 * tile_size : 4 * tile_size])
    back_terms = jnp.einsum(
        "kab,kaf->kbf",
        off_tiles,
        jnp.take(own_blocks, off_row, axis=0),
        preferred_element_type=jnp.float32,
    ).astype(jnp.bfloat16)
    outgoing = serve_blocks(pages)
    fetched = lax.all_to_all(outgoing, "band", split_axis=0, concat_axis=0, tiled=True)
    returned = lax.all_to_all(back_terms, "band", split_axis=0, concat_axis=0, tiled=True)
    prop_a = (near_part + off_apply(fetched)).reshape(rows_dev, feat_half).astype(jnp.bfloat16)
    back_sum = jnp.einsum(
        "rk,kbf->rbf", served_hot, returned.astype(jnp.float32), precision=lax.Precision.HIGHEST
    )
    prop_t = (inner_part + back_sum).reshape(rows_dev, feat_half).astype(jnp.bfloat16)
    fetched_again = lax.all_to_all(
        serve_blocks(prop_t), "band", split_axis=0, concat_axis=0, tiled=True
    )
    prop_aat = (
        (band_forward(prop_t) + off_apply(fetched_again))
        .reshape(rows_dev, feat_half)
        .astype(jnp.bfloat16)
    )
    picked = jnp.stack(
        [
            jnp.take(prop_a, label_page, axis=0),
            jnp.take(prop_t, label_page, axis=0),
            jnp.take(prop_aat, label_page, axis=0),
        ],
        0,
    )
    regrouped = lax.all_to_all(picked, "dp", split_axis=1, concat_axis=2, tiled=True)
    hidden_units = w_first.shape[1]
    w_first_split = w_first.reshape(3, regrouped.shape[2], hidden_units)
    pre_act = jnp.einsum(
        "krf,kfh->rh", regrouped, w_first_split, preferred_element_type=jnp.float32
    )
    sigma = jax.nn.sigmoid(pre_act)
    hidden = (pre_act * sigma).astype(jnp.bfloat16)
    logits = jnp.dot(hidden, w_second, preferred_element_type=jnp.float32)
    probabilities = jax.nn.softmax(logits, axis=-1)
    label_hot = (labels[:, None] == jnp.arange(w_second.shape[1], dtype=jnp.int32)[None, :]).astype(
        jnp.float32
    )
    errors = ((probabilities - label_hot) / label_page.shape[0]).astype(jnp.bfloat16)
    grad_second = jnp.dot(hidden.T, errors, preferred_element_type=jnp.float32)
    slope = sigma * (1.0 + pre_act * (1.0 - sigma))
    back_signal = (jnp.dot(errors, w_second.T, preferred_element_type=jnp.float32) * slope).astype(
        jnp.bfloat16
    )
    grad_first = jnp.einsum(
        "krf,rh->kfh", regrouped, back_signal, preferred_element_type=jnp.float32
    ).reshape(w_first.shape[0], hidden_units)
    summed_first, summed_second = summed_gradients(grad_first, grad_second)
    return (
        prop_a,
        prop_t,
        prop_aat,
        summed_first,
        summed_second,
    )


def solution(mesh):
    placed = (
        P("band", "dp"),
        P("band", None, None, None),
        P("band", None, None),
        P("band"),
        P("band"),
        P("band"),
        P(("band", "dp")),
        P(),
        P(),
    )
    return jax.shard_map(
        per_device,
        mesh=mesh,
        in_specs=placed,
        out_specs=(P("band", "dp"), P("band", "dp"), P("band", "dp"), P(), P()),
        check_vma=False,
    )
```

```python
import functools

import jax
import jax.numpy as jnp
from jax import lax
from jax.experimental import pallas as pl
from jax.experimental.pallas import tpu as pltpu
from jax.sharding import PartitionSpec as P


MESH = pl.DeviceIdType.MESH


def greet_all(n):
    b, other = lax.axis_index("band"), 1 - lax.axis_index("dp")
    barrier = pltpu.get_barrier_semaphore()
    pl.semaphore_signal(barrier, inc=1, device_id={"dp": other}, device_id_type=MESH)

    def greet(d, _):
        pl.semaphore_signal(
            barrier, inc=1, device_id={"band": lax.rem(b + d, n)}, device_id_type=MESH
        )
        return 0

    lax.fori_loop(1, n, greet, 0)
    pl.semaphore_wait(barrier, n)


def remote(src, dst, send_sem, recv_sem, **where):
    return pltpu.make_async_remote_copy(
        src_ref=src, dst_ref=dst, send_sem=send_sem, recv_sem=recv_sem,
        device_id=where, device_id_type=MESH,
    )


def each(start, stop, body):
    def step(d, _):
        body(d)
        return 0

    lax.fori_loop(start, stop, step, 0)


def reduce_kernel(
    n, cols, g1, g2, out, recv1, recv2, send, land, acc,
    s_core, r_core, s_rs, r_rs, s_ag, r_ag, s_fw, r_fw,
):
    b, h = lax.axis_index("band"), lax.axis_index("dp")
    o = 1 - h
    width = send.shape[2] // cols
    top = recv1.shape[0]
    step_rows = send.shape[1]
    quarter = recv2.shape[0] // 4
    wide = recv2.shape[1]

    def part(c):
        return lax.div(c, cols), pl.ds(pl.multiple_of(lax.rem(c, cols) * width, 128), width)

    greet_all(n)
    first = remote(g1.at[o], recv1, s_core.at[0], r_core.at[0], dp=o)
    second = remote(g2.at[o], recv2, s_core.at[1], r_core.at[1], dp=o)
    first.start()
    second.start()
    first.wait()

    def fill_first(i):
        rows = pl.ds(pl.multiple_of(i * step_rows, step_rows), step_rows)
        send[i] = (g1[h, rows] + recv1[rows]).astype(jnp.bfloat16)

    each(0, top // step_rows, fill_first)
    second.wait()

    def fill_second(i):
        for j in range(4):
            rows = pl.ds(pl.multiple_of(j * quarter + i * step_rows, step_rows), step_rows)
            send[top // step_rows + i, :, j * wide : (j + 1) * wide] = (
                g2[h, rows] + recv2[rows]
            ).astype(jnp.bfloat16)

    each(0, quarter // step_rows, fill_second)

    def scatter(d):
        t = lax.rem(b + d, n)
        i, w = part(t)
        return remote(send.at[i, :, w], land.at[d], s_rs.at[d], r_rs.at[d], band=t)

    each(1, n, lambda d: scatter(d).start())
    mine, mine_w = part(b)
    acc[...] = send[mine, :, mine_w].astype(jnp.float32)

    def collect(d):
        scatter(d).wait_recv()
        acc[...] += land[d].astype(jnp.float32)

    each(1, n, collect)
    out[h, mine, :, mine_w] = acc[...].astype(jnp.bfloat16)

    def spread(d):
        spot = out.at[h, mine, :, mine_w]
        return remote(spot, spot, s_ag.at[d], r_ag.at[d], band=lax.rem(b + d, n))

    def arrival(d):
        i, w = part(lax.rem(b + n - d, n))
        spot = out.at[h, i, :, w]
        return remote(spot, spot, s_ag.at[d], r_ag.at[d], band=lax.rem(b + d, n))

    def forward(d):
        i, w = part(lax.rem(b + n - d, n))
        spot = out.at[h, i, :, w]
        return remote(spot, spot, s_fw.at[d], r_fw.at[d], dp=o)

    def forwarded(d):
        i, w = part(lax.rem(b + n - d, n))
        spot = out.at[o, i, :, w]
        return remote(spot, spot, s_fw.at[d], r_fw.at[d], dp=o)

    each(1, n, lambda d: spread(d).start())
    forward(0).start()

    def pass_on(d):
        arrival(d).wait_recv()
        forward(d).start()

    each(1, n, pass_on)

    def finish(d):
        scatter(d).wait_send()
        spread(d).wait_send()

    each(1, n, finish)

    def finish_pair(d):
        forward(d).wait_send()
        forwarded(d).wait_recv()

    each(0, n, finish_pair)


def summed_gradients(grad_first, grad_second):
    n = lax.axis_size("band")
    cols = max(1, n // 16)
    in_f, hid = grad_first.shape
    classes = grad_second.shape[1]
    half_rows = (grad_first.size + grad_second.size) // (2 * hid)
    step_rows = half_rows * cols // n
    blocks = half_rows // step_rows
    top = in_f // 2
    vmem = pl.BlockSpec(memory_space=pltpu.VMEM)
    dma = pltpu.SemaphoreType.DMA
    packed = pl.pallas_call(
        functools.partial(reduce_kernel, n, cols),
        out_shape=jax.ShapeDtypeStruct((2, blocks, step_rows, hid), jnp.bfloat16),
        in_specs=[vmem] * 2,
        out_specs=vmem,
        scratch_shapes=[
            pltpu.VMEM((top, hid), jnp.float32),
            pltpu.VMEM((hid // 2, classes), jnp.float32),
            pltpu.VMEM((blocks, step_rows, hid), jnp.bfloat16),
            pltpu.VMEM((n, step_rows, hid // cols), jnp.bfloat16),
            pltpu.VMEM((step_rows, hid // cols), jnp.float32),
            dma((2,)), dma((2,)), dma((n,)), dma((n,)), dma((n,)), dma((n,)), dma((n,)), dma((n,)),
        ],
        compiler_params=pltpu.CompilerParams(
            collective_id=0, has_side_effects=True, vmem_limit_bytes=40 * 2**20
        ),
        name="grad_sum",
    )(grad_first.reshape(2, top, hid), grad_second.reshape(2, hid // 2, classes))
    packed = packed.reshape(2, half_rows, hid)
    parts = hid // classes
    low = packed[:, top:].reshape(2, half_rows - top, parts, classes)
    return (
        packed[:, :top].reshape(in_f, hid),
        low.transpose(0, 2, 1, 3).reshape(hid, classes),
    )


def propagate_kernel(
    n, pages, tiles, offs, off_row, req, label, prop_a, prop_t, prop_aat, feats,
    hot, back_send, back_land, page_send, page_land, t_send, t_land, pad, padt,
    rim_send, rim_land, inner, acc, req_land, served, sel, local_sem,
    s_req, r_req, s_back, r_back, s_page, r_page, s_t, r_t, s_edge, r_edge, s_pick, r_pick,
):
    b, h = lax.axis_index("band"), lax.axis_index("dp")
    o = 1 - h
    nb, tile, fh = pages.shape
    left, right = lax.rem(b + n - 1, n), lax.rem(b + 1, n)
    half = feats.shape[0]
    f32, bf16 = jnp.float32, jnp.bfloat16

    def ahead(d):
        return lax.rem(b + d, n)

    def behind(d):
        return lax.rem(b + n - d, n)

    def tdot(x, y):
        return lax.dot_general(x, y, (((0,), (0,)), ((), ())), preferred_element_type=f32)

    def dot(x, y):
        return jnp.dot(x, y, preferred_element_type=f32)

    barrier = pltpu.get_barrier_semaphore()
    pl.semaphore_signal(barrier, inc=1, device_id={"dp": o}, device_id_type=MESH)
    each(
        1,
        n,
        lambda d: pl.semaphore_signal(
            barrier, inc=1, device_id={"band": ahead(d)}, device_id_type=MESH
        ),
    )
    chunk = 128
    page_iota = lax.broadcasted_iota(jnp.int32, (chunk, nb * tile), 1)

    def build_hot(i):
        rows = pl.ds(pl.multiple_of(i * chunk, chunk), chunk)
        hot[rows] = jnp.where(label[rows] == page_iota, 1.0, 0.0).astype(bf16)

    each(0, hot.shape[0] // chunk, build_hot)
    rim_send[0] = tdot(tiles[0, 0], pages[0])
    rim_send[1] = tdot(tiles[nb - 1, 2], pages[nb - 1])
    pl.semaphore_wait(barrier, n)

    def ask(d):
        t = ahead(d)
        return remote(req.at[t], req_land.at[d], s_req.at[d], r_req.at[d], band=t)

    def send_back(d):
        return remote(back_send.at[d], back_land.at[d], s_back.at[d], r_back.at[d], band=ahead(d))

    def send_page(d):
        return remote(page_send.at[d], page_land.at[d], s_page.at[d], r_page.at[d], band=behind(d))

    def send_t(d):
        return remote(t_send.at[d], t_land.at[d], s_t.at[d], r_t.at[d], band=behind(d))

    def edges(source, field, i):
        first, last = source
        return (
            remote(first, field.at[nb + 1], s_edge.at[i], r_edge.at[i], band=left),
            remote(last, field.at[0], s_edge.at[i + 1], r_edge.at[i + 1], band=right),
        )

    each(1, n, lambda d: ask(d).start())
    rims = (
        remote(rim_send.at[0], rim_land.at[0], s_edge.at[2], r_edge.at[2], band=left),
        remote(rim_send.at[1], rim_land.at[1], s_edge.at[3], r_edge.at[3], band=right),
    )
    page_edges = edges((pages.at[0], pages.at[nb - 1]), pad, 0)
    for copy in rims + page_edges:
        copy.start()

    def back_term(d):
        k = ahead(d)
        return tdot(offs[k], pages[off_row[k]]).astype(bf16)

    def make_back(d):
        back_send[d] = back_term(d)
        send_back(d).start()

    each(1, n, make_back)
    back_land[0] = back_term(0)
    req_land[0] = req[b]
    each(1, n, lambda d: ask(d).wait_recv())
    to_scalar = pltpu.make_async_copy(req_land, served, local_sem.at[0])
    to_scalar.start()
    to_scalar.wait()

    def make_page(d):
        page_send[d] = pages[served[d, 0, 0]]
        send_page(d).start()

    each(1, n, make_page)
    page_land[0] = pages[served[0, 0, 0]]

    inner[0] = tdot(tiles[0, 1], pages[0]) + tdot(tiles[1, 0], pages[1])
    inner[nb - 1] = tdot(tiles[nb - 1, 1], pages[nb - 1]) + tdot(tiles[nb - 2, 2], pages[nb - 2])

    def adjoint(m):
        inner[m] = (
            tdot(tiles[m - 1, 2], pages[m - 1])
            + tdot(tiles[m, 1], pages[m])
            + tdot(tiles[m + 1, 0], pages[m + 1])
        )

    each(1, nb - 1, adjoint)
    for copy in rims:
        copy.wait()
    inner[nb - 1] += jnp.where(b < n - 1, 1.0, 0.0) * rim_land[0]
    inner[0] += jnp.where(b > 0, 1.0, 0.0) * rim_land[1]

    def spread_rows(target, spot, term):
        for r in range(nb):
            target[r] += jnp.where(spot == r, 1.0, 0.0) * term

    def take_back(d):
        spread_rows(inner, served[d, 0, 0], back_land[d].astype(f32))

    take_back(0)

    def await_back(d):
        send_back(d).wait_recv()
        take_back(d)

    each(1, n, await_back)

    def round_t(r):
        block = inner[r].astype(bf16)
        padt[r + 1] = block
        prop_t[r] = block

    each(0, nb, round_t)
    t_edges = edges((padt.at[1], padt.at[nb]), padt, 4)
    for copy in t_edges:
        copy.start()

    def make_t(d):
        t_send[d] = prop_t[served[d, 0, 0]]
        send_t(d).start()

    each(1, n, make_t)
    t_land[0] = prop_t[served[0, 0, 0]]

    def copy_pages(r):
        pad[r + 1] = pages[r]

    each(0, nb, copy_pages)

    def clear_ends(field):
        @pl.when(b == 0)
        def _():
            field[0] = jnp.zeros((tile, fh), bf16)

        @pl.when(b == n - 1)
        def _():
            field[nb + 1] = jnp.zeros((tile, fh), bf16)

    def near(field):
        def row(r):
            weights = jnp.concatenate([tiles[r, 0], tiles[r, 1], tiles[r, 2]], axis=1)
            window = jnp.concatenate([field[r], field[r + 1], field[r + 2]], axis=0)
            acc[r] = dot(weights, window)

        each(0, nb, row)

    def take_off(land, d):
        k = ahead(d)
        spread_rows(acc, off_row[k], dot(offs[k], land[d]))

    def pick(j, field):
        whole = field[1 : nb + 1].reshape(nb * tile, fh)
        step = half // 2

        def rows_of(core, c):
            return pl.ds(pl.multiple_of(core * half + c * step, step), step)

        columns = pl.ds(pl.multiple_of((2 * j + h) * fh, fh), fh)
        for c in range(2):
            sel[j, c * step : (c + 1) * step] = dot(hot[rows_of(o, c)], whole).astype(bf16)
        give = remote(sel.at[j], feats.at[:, columns], s_pick.at[j], r_pick.at[j], dp=o)
        give.start()
        for c in range(2):
            feats[c * step : (c + 1) * step, columns] = dot(hot[rows_of(h, c)], whole).astype(bf16)
        return give

    gives = [pick(1, padt)]
    for copy in page_edges:
        copy.wait()
    clear_ends(pad)
    near(pad)
    take_off(page_land, 0)

    def await_page(d):
        send_page(d).wait_recv()
        take_off(page_land, d)

    each(1, n, await_page)

    def round_a(r):
        block = acc[r].astype(bf16)
        pad[r + 1] = block
        prop_a[r] = block

    each(0, nb, round_a)
    gives.append(pick(0, pad))
    for copy in t_edges:
        copy.wait()
    clear_ends(padt)
    near(padt)
    take_off(t_land, 0)

    def await_t(d):
        send_t(d).wait_recv()
        take_off(t_land, d)

    each(1, n, await_t)

    def round_aat(r):
        block = acc[r].astype(bf16)
        padt[r + 1] = block
        prop_aat[r] = block

    each(0, nb, round_aat)
    gives.append(pick(2, padt))

    def finish(d):
        ask(d).wait_send()
        send_back(d).wait_send()
        send_page(d).wait_send()
        send_t(d).wait_send()

    each(1, n, finish)
    for j, give in zip((1, 0, 2), gives):
        give.wait_send()
        columns = pl.ds(pl.multiple_of((2 * j + o) * fh, fh), fh)
        remote(
            sel.at[j], feats.at[:, columns], s_pick.at[j], r_pick.at[j], dp=o
        ).wait_recv()


def propagated(pages, band_tiles, off_tiles, off_row, requests, label_page):
    n = lax.axis_size("band")
    tile = band_tiles.shape[-1]
    rows, fh = pages.shape
    nb = rows // tile
    count = label_page.shape[0]
    bf16, f32 = jnp.bfloat16, jnp.float32
    vmem = pl.BlockSpec(memory_space=pltpu.VMEM)
    smem = pl.BlockSpec(memory_space=pltpu.SMEM)
    dma = pltpu.SemaphoreType.DMA
    blocks = jax.ShapeDtypeStruct((nb, tile, fh), bf16)
    per_band = pltpu.VMEM((n, tile, fh), bf16)
    padded = pltpu.VMEM((nb + 2, tile, fh), bf16)
    prop_a, prop_t, prop_aat, feats = pl.pallas_call(
        functools.partial(propagate_kernel, n),
        out_shape=(blocks, blocks, blocks, jax.ShapeDtypeStruct((count // 2, 6 * fh), bf16)),
        in_specs=[vmem, vmem, vmem, smem, vmem, vmem],
        out_specs=(vmem,) * 4,
        scratch_shapes=[
            pltpu.VMEM((count, rows), bf16),
            per_band, per_band, per_band, per_band, per_band, per_band,
            padded, padded,
            pltpu.VMEM((2, tile, fh), f32),
            pltpu.VMEM((2, tile, fh), f32),
            pltpu.VMEM((nb, tile, fh), f32),
            pltpu.VMEM((nb, tile, fh), f32),
            pltpu.VMEM((n, 1, 128), jnp.int32),
            pltpu.SMEM((n, 1, 128), jnp.int32),
            pltpu.VMEM((3, count // 2, fh), bf16),
            dma((1,)),
            *([dma((n,))] * 8), dma((6,)), dma((6,)), dma((3,)), dma((3,)),
        ],
        compiler_params=pltpu.CompilerParams(
            collective_id=1, has_side_effects=True, vmem_limit_bytes=56 * 2**20
        ),
        name="propagate",
    )(
        pages.reshape(nb, tile, fh),
        band_tiles,
        off_tiles,
        off_row,
        jnp.broadcast_to(requests[:, None, None], (n, 1, 128)),
        label_page[:, None],
    )
    return prop_a.reshape(rows, fh), prop_t.reshape(rows, fh), prop_aat.reshape(rows, fh), feats


def per_device(
    pages, band_tiles, off_tiles, off_row, requests, label_page, labels, w_first, w_second
):
    prop_a, prop_t, prop_aat, features = propagated(
        pages, band_tiles, off_tiles, off_row, requests, label_page
    )
    pre_act = jnp.dot(features, w_first, preferred_element_type=jnp.float32)
    sigma = jax.nn.sigmoid(pre_act)
    hidden = (pre_act * sigma).astype(jnp.bfloat16)
    logits = jnp.dot(hidden, w_second, preferred_element_type=jnp.float32)
    probabilities = jax.nn.softmax(logits, axis=-1)
    label_hot = (labels[:, None] == jnp.arange(w_second.shape[1], dtype=jnp.int32)[None, :]).astype(
        jnp.float32
    )
    errors = ((probabilities - label_hot) / label_page.shape[0]).astype(jnp.bfloat16)
    grad_second = jnp.dot(hidden.T, errors, preferred_element_type=jnp.float32)
    slope = sigma * (1.0 + pre_act * (1.0 - sigma))
    back_signal = (jnp.dot(errors, w_second.T, preferred_element_type=jnp.float32) * slope).astype(
        jnp.bfloat16
    )
    grad_first = jnp.dot(features.T, back_signal, preferred_element_type=jnp.float32)
    summed_first, summed_second = summed_gradients(grad_first, grad_second)
    return (
        prop_a,
        prop_t,
        prop_aat,
        summed_first,
        summed_second,
    )


def solution(mesh):
    placed = (
        P("band", "dp"),
        P("band", None, None, None),
        P("band", None, None),
        P("band"),
        P("band"),
        P("band"),
        P(("band", "dp")),
        P(),
        P(),
    )
    return jax.shard_map(
        per_device,
        mesh=mesh,
        in_specs=placed,
        out_specs=(P("band", "dp"), P("band", "dp"), P("band", "dp"), P(), P()),
        check_vma=False,
    )
```

```python
import functools

import jax
import jax.numpy as jnp
from jax import lax
from jax.experimental import pallas as pl
from jax.experimental.pallas import tpu as pltpu
from jax.sharding import PartitionSpec as P


MESH = pl.DeviceIdType.MESH


def greet_all(n):
    b, other = lax.axis_index("band"), 1 - lax.axis_index("dp")
    barrier = pltpu.get_barrier_semaphore()
    pl.semaphore_signal(barrier, inc=1, device_id={"dp": other}, device_id_type=MESH)

    def greet(d, _):
        pl.semaphore_signal(
            barrier, inc=1, device_id={"band": lax.rem(b + d, n)}, device_id_type=MESH
        )
        return 0

    lax.fori_loop(1, n, greet, 0)
    pl.semaphore_wait(barrier, n)


def remote(src, dst, send_sem, recv_sem, **where):
    return pltpu.make_async_remote_copy(
        src_ref=src, dst_ref=dst, send_sem=send_sem, recv_sem=recv_sem,
        device_id=where, device_id_type=MESH,
    )


def each(start, stop, body):
    def step(d, _):
        body(d)
        return 0

    lax.fori_loop(start, stop, step, 0)


def reduce_kernel(
    g, depth, pieces, g1, g2, out, recv1, recv2, cur, land1, land2, land3,
    s_core, r_core, s_one, r_one, s_two, r_two, s_z, r_z,
    s_gz, r_gz, s_g2, r_g2, s_g1, r_g1, s_fw, r_fw,
):
    n = g * g * depth
    b, h = lax.axis_index("band"), lax.axis_index("dp")
    o = 1 - h
    x, y, z = lax.rem(b, g), lax.rem(lax.div(b, g), g), lax.div(b, g * g)
    c1, c2 = x + h * (y - x), y + h * (x - y)
    stride1, stride2 = 1 + h * (g - 1), g - h * (g - 1)
    top, hid = recv1.shape
    low, classes = recv2.shape
    half = out.shape[1]
    quarter = half - top
    rows1 = half // g
    rows2 = rows1 // g
    width = hid // pieces
    thin = width // depth
    low_step = low // pieces
    base1 = c1 * rows1
    base2 = base1 + c2 * rows2
    chunk = 32

    def down(start, size):
        return pl.ds(pl.multiple_of(start, chunk), size)

    def across(start, size):
        return pl.ds(pl.multiple_of(start, 128), size)

    def member1(d):
        m = lax.rem(c1 + d, g)
        return m, b + (m - c1) * stride1

    def member2(d):
        m = lax.rem(c2 + d, g)
        return m, b + (m - c2) * stride2

    def member_z(d):
        m = lax.rem(z + d, depth)
        return m, b + (m - z) * (g * g)

    def core_copies(p):
        w, r = pl.ds(p * width, width), pl.ds(p * low_step, low_step)
        return (
            remote(g1.at[o, :, w], recv1.at[:, w], s_core.at[p, 0], r_core.at[p, 0], dp=o),
            remote(g2.at[o, r], recv2.at[r], s_core.at[p, 1], r_core.at[p, 1], dp=o),
        )

    def one(p, d):
        m, t = member1(d)
        src = cur.at[down(m * rows1, rows1), pl.ds(p * width, width)]
        return remote(src, land1.at[p, d - 1], s_one.at[p, d - 1], r_one.at[p, d - 1], band=t)

    def two(p, d):
        m, t = member2(d)
        src = cur.at[down(base1 + m * rows2, rows2), pl.ds(p * width, width)]
        return remote(src, land2.at[p, d - 1], s_two.at[p, d - 1], r_two.at[p, d - 1], band=t)

    def along_z(p, d):
        m, t = member_z(d)
        src = cur.at[down(base2, rows2), across(p * width + m * thin, thin)]
        return remote(src, land3.at[p, d - 1], s_z.at[p, d - 1], r_z.at[p, d - 1], band=t)

    def back_z(p, d, taking=False):
        m, t = member_z(d)
        owner = lax.rem(z + depth - d, depth) if taking else z
        spot = out.at[h, down(base2, rows2), across(p * width + owner * thin, thin)]
        return remote(spot, spot, s_gz.at[p, d - 1], r_gz.at[p, d - 1], band=t)

    def back2(p, d, taking=False):
        m, t = member2(d)
        owner = lax.rem(c2 + g - d, g) if taking else c2
        spot = out.at[h, down(base1 + owner * rows2, rows2), pl.ds(p * width, width)]
        return remote(spot, spot, s_g2.at[p, d - 1], r_g2.at[p, d - 1], band=t)

    def back1(p, d, taking=False):
        m, t = member1(d)
        owner = lax.rem(c1 + g - d, g) if taking else c1
        spot = out.at[h, down(owner * rows1, rows1), pl.ds(p * width, width)]
        return remote(spot, spot, s_g1.at[p, d - 1], r_g1.at[p, d - 1], band=t)

    def forward(p, core):
        spot = out.at[core, :, pl.ds(p * width, width)]
        return remote(spot, spot, s_fw.at[p], r_fw.at[p], dp=o)

    def begin(p):
        w = pl.ds(p * width, width)
        first, second = core_copies(p)
        first.wait_recv()

        def add_top(i):
            rows = down(i * chunk, chunk)
            cur[rows, w] = g1[h, rows, w] + recv1[rows, w]

        each(0, top // chunk, add_top)
        second.wait_recv()

        def add_low(i):
            for j in range(low_step // quarter):
                rows = down(p * low_step + j * quarter + i * chunk, chunk)
                place = pl.ds(p * width + j * classes, classes)
                cur[down(top + i * chunk, chunk), place] = g2[h, rows] + recv2[rows]

        each(0, quarter // chunk, add_low)
        for d in range(1, g):
            one(p, d).start()

    def gather_in(copies, p, base, rows, land, w):
        for copy in copies:
            copy.wait_recv()

        def add(i):
            spot = down(base + i * chunk, chunk)
            total = cur[spot, w]
            for m in range(len(copies)):
                total += land[p, m, down(i * chunk, chunk)]
            cur[spot, w] = total

        if copies:
            each(0, rows // chunk, add)

    def after_one(p):
        gather_in([one(p, d) for d in range(1, g)], p, base1, rows1, land1, pl.ds(p * width, width))
        for d in range(1, g):
            two(p, d).start()

    def after_two(p):
        gather_in([two(p, d) for d in range(1, g)], p, base2, rows2, land2, pl.ds(p * width, width))
        for d in range(1, depth):
            along_z(p, d).start()

    def after_z(p):
        w = across(p * width + z * thin, thin)
        gather_in([along_z(p, d) for d in range(1, depth)], p, base2, rows2, land3, w)

        def settle(i):
            rows = down(base2 + i * chunk, chunk)
            out[h, rows, w] = cur[rows, w].astype(jnp.bfloat16)

        each(0, rows2 // chunk, settle)
        for d in range(1, depth):
            back_z(p, d).start()

    def after_back_z(p):
        for d in range(1, depth):
            back_z(p, d, True).wait_recv()
        for d in range(1, g):
            back2(p, d).start()

    def after_back2(p):
        for d in range(1, g):
            back2(p, d, True).wait_recv()
        for d in range(1, g):
            back1(p, d).start()

    def after_back1(p):
        for d in range(1, g):
            back1(p, d, True).wait_recv()
        forward(p, h).start()

    greet_all(n)
    for p in range(pieces):
        for copy in core_copies(p):
            copy.start()
    stages = (begin, after_one, after_two, after_z, after_back_z, after_back2, after_back1)
    for t in range(len(stages) + pieces - 1):
        for p in reversed(range(pieces)):
            if 0 <= t - p < len(stages):
                stages[t - p](p)
    for p in range(pieces):
        for copy in core_copies(p):
            copy.wait_send()
        for d in range(1, g):
            for copy in (one(p, d), two(p, d), back2(p, d), back1(p, d)):
                copy.wait_send()
        for d in range(1, depth):
            along_z(p, d).wait_send()
            back_z(p, d).wait_send()
        forward(p, h).wait_send()
        forward(p, o).wait_recv()


def summed_gradients(grad_first, grad_second):
    n = lax.axis_size("band")
    g = max(1, round((n / 2) ** (1 / 3)))
    if n % (g * g):
        g = 1
    depth = n // (g * g)
    in_f, hid = grad_first.shape
    classes = grad_second.shape[1]
    top, low = in_f // 2, hid // 2
    half = (grad_first.size + grad_second.size) // (2 * hid)
    pieces = max(1, hid // (128 * depth))
    width = hid // pieces
    f32 = jnp.float32
    vmem = pl.BlockSpec(memory_space=pltpu.VMEM)
    dma = pltpu.SemaphoreType.DMA
    side, deep = max(1, g - 1), max(1, depth - 1)
    near, far = dma((pieces, side)), dma((pieces, deep))
    packed = pl.pallas_call(
        functools.partial(reduce_kernel, g, depth, pieces),
        out_shape=jax.ShapeDtypeStruct((2, half, hid), jnp.bfloat16),
        in_specs=[vmem] * 2,
        out_specs=vmem,
        scratch_shapes=[
            pltpu.VMEM((top, hid), f32),
            pltpu.VMEM((low, classes), f32),
            pltpu.VMEM((half, hid), f32),
            pltpu.VMEM((pieces, side, half // g, width), f32),
            pltpu.VMEM((pieces, side, half // (g * g), width), f32),
            pltpu.VMEM((pieces, deep, half // (g * g), width // depth), f32),
            dma((pieces, 2)), dma((pieces, 2)),
            near, near, near, near, far, far, far, far, near, near, near, near,
            dma((pieces,)), dma((pieces,)),
        ],
        compiler_params=pltpu.CompilerParams(
            collective_id=0, has_side_effects=True, vmem_limit_bytes=40 * 2**20
        ),
        name="grad_sum",
    )(grad_first.reshape(2, top, hid), grad_second.reshape(2, low, classes))
    parts = hid // classes
    rest = packed[:, top:].reshape(2, half - top, parts, classes)
    return (
        packed[:, :top].reshape(in_f, hid),
        rest.transpose(0, 2, 1, 3).reshape(hid, classes),
    )


def propagate_kernel(
    n, pages, tiles, offs, off_row, req, label, prop_a, prop_t, prop_aat, feats,
    hot, back_send, back_land, page_send, page_land, t_send, t_land, pad, padt,
    rim_send, rim_land, inner, acc, req_land, served, sel, local_sem,
    s_req, r_req, s_back, r_back, s_page, r_page, s_t, r_t, s_edge, r_edge, s_pick, r_pick,
):
    b, h = lax.axis_index("band"), lax.axis_index("dp")
    o = 1 - h
    nb, tile, fh = pages.shape
    left, right = lax.rem(b + n - 1, n), lax.rem(b + 1, n)
    half = feats.shape[0]
    f32, bf16 = jnp.float32, jnp.bfloat16

    def ahead(d):
        return lax.rem(b + d, n)

    def behind(d):
        return lax.rem(b + n - d, n)

    def tdot(x, y):
        return lax.dot_general(x, y, (((0,), (0,)), ((), ())), preferred_element_type=f32)

    def dot(x, y):
        return jnp.dot(x, y, preferred_element_type=f32)

    barrier = pltpu.get_barrier_semaphore()
    pl.semaphore_signal(barrier, inc=1, device_id={"dp": o}, device_id_type=MESH)
    each(
        1,
        n,
        lambda d: pl.semaphore_signal(
            barrier, inc=1, device_id={"band": ahead(d)}, device_id_type=MESH
        ),
    )
    chunk = 128
    page_iota = lax.broadcasted_iota(jnp.int32, (chunk, nb * tile), 1)

    def build_hot(i):
        rows = pl.ds(pl.multiple_of(i * chunk, chunk), chunk)
        hot[rows] = jnp.where(label[rows] == page_iota, 1.0, 0.0).astype(bf16)

    each(0, hot.shape[0] // chunk, build_hot)
    rim_send[0] = tdot(tiles[0, 0], pages[0])
    rim_send[1] = tdot(tiles[nb - 1, 2], pages[nb - 1])
    pl.semaphore_wait(barrier, n)

    def ask(d):
        t = ahead(d)
        return remote(req.at[t], req_land.at[d], s_req.at[d], r_req.at[d], band=t)

    def send_back(d):
        return remote(back_send.at[d], back_land.at[d], s_back.at[d], r_back.at[d], band=ahead(d))

    def send_page(d):
        return remote(page_send.at[d], page_land.at[d], s_page.at[d], r_page.at[d], band=behind(d))

    def send_t(d):
        return remote(t_send.at[d], t_land.at[d], s_t.at[d], r_t.at[d], band=behind(d))

    def edges(source, field, i):
        first, last = source
        return (
            remote(first, field.at[nb + 1], s_edge.at[i], r_edge.at[i], band=left),
            remote(last, field.at[0], s_edge.at[i + 1], r_edge.at[i + 1], band=right),
        )

    each(1, n, lambda d: ask(d).start())
    rims = (
        remote(rim_send.at[0], rim_land.at[0], s_edge.at[2], r_edge.at[2], band=left),
        remote(rim_send.at[1], rim_land.at[1], s_edge.at[3], r_edge.at[3], band=right),
    )
    page_edges = edges((pages.at[0], pages.at[nb - 1]), pad, 0)
    for copy in rims + page_edges:
        copy.start()

    def back_term(d):
        k = ahead(d)
        return tdot(offs[k], pages[off_row[k]]).astype(bf16)

    def make_back(d):
        back_send[d] = back_term(d)
        send_back(d).start()

    each(1, n, make_back)
    back_land[0] = back_term(0)
    req_land[0] = req[b]
    each(1, n, lambda d: ask(d).wait_recv())
    to_scalar = pltpu.make_async_copy(req_land, served, local_sem.at[0])
    to_scalar.start()
    to_scalar.wait()

    def make_page(d):
        page_send[d] = pages[served[d, 0, 0]]
        send_page(d).start()

    each(1, n, make_page)
    page_land[0] = pages[served[0, 0, 0]]

    inner[0] = tdot(tiles[0, 1], pages[0]) + tdot(tiles[1, 0], pages[1])
    inner[nb - 1] = tdot(tiles[nb - 1, 1], pages[nb - 1]) + tdot(tiles[nb - 2, 2], pages[nb - 2])

    def adjoint(m):
        inner[m] = (
            tdot(tiles[m - 1, 2], pages[m - 1])
            + tdot(tiles[m, 1], pages[m])
            + tdot(tiles[m + 1, 0], pages[m + 1])
        )

    each(1, nb - 1, adjoint)
    for copy in rims:
        copy.wait()
    inner[nb - 1] += jnp.where(b < n - 1, 1.0, 0.0) * rim_land[0]
    inner[0] += jnp.where(b > 0, 1.0, 0.0) * rim_land[1]

    def spread_rows(target, spot, term):
        for r in range(nb):
            target[r] += jnp.where(spot == r, 1.0, 0.0) * term

    def take_back(d):
        spread_rows(inner, served[d, 0, 0], back_land[d].astype(f32))

    take_back(0)

    def await_back(d):
        send_back(d).wait_recv()
        take_back(d)

    each(1, n, await_back)

    def round_t(r):
        block = inner[r].astype(bf16)
        padt[r + 1] = block
        prop_t[r] = block

    each(0, nb, round_t)
    t_edges = edges((padt.at[1], padt.at[nb]), padt, 4)
    for copy in t_edges:
        copy.start()

    def make_t(d):
        t_send[d] = prop_t[served[d, 0, 0]]
        send_t(d).start()

    each(1, n, make_t)
    t_land[0] = prop_t[served[0, 0, 0]]

    def copy_pages(r):
        pad[r + 1] = pages[r]

    each(0, nb, copy_pages)

    def clear_ends(field):
        @pl.when(b == 0)
        def _():
            field[0] = jnp.zeros((tile, fh), bf16)

        @pl.when(b == n - 1)
        def _():
            field[nb + 1] = jnp.zeros((tile, fh), bf16)

    def near(field):
        def row(r):
            weights = jnp.concatenate([tiles[r, 0], tiles[r, 1], tiles[r, 2]], axis=1)
            window = jnp.concatenate([field[r], field[r + 1], field[r + 2]], axis=0)
            acc[r] = dot(weights, window)

        each(0, nb, row)

    def take_off(land, d):
        k = ahead(d)
        spread_rows(acc, off_row[k], dot(offs[k], land[d]))

    def pick(j, field):
        whole = field[1 : nb + 1].reshape(nb * tile, fh)
        step = half // 2

        def rows_of(core, c):
            return pl.ds(pl.multiple_of(core * half + c * step, step), step)

        columns = pl.ds(pl.multiple_of((2 * j + h) * fh, fh), fh)
        for c in range(2):
            sel[j, c * step : (c + 1) * step] = dot(hot[rows_of(o, c)], whole).astype(bf16)
        give = remote(sel.at[j], feats.at[:, columns], s_pick.at[j], r_pick.at[j], dp=o)
        give.start()
        for c in range(2):
            feats[c * step : (c + 1) * step, columns] = dot(hot[rows_of(h, c)], whole).astype(bf16)
        return give

    gives = [pick(1, padt)]
    for copy in page_edges:
        copy.wait()
    clear_ends(pad)
    near(pad)
    take_off(page_land, 0)

    def await_page(d):
        send_page(d).wait_recv()
        take_off(page_land, d)

    each(1, n, await_page)

    def round_a(r):
        block = acc[r].astype(bf16)
        pad[r + 1] = block
        prop_a[r] = block

    each(0, nb, round_a)
    gives.append(pick(0, pad))
    for copy in t_edges:
        copy.wait()
    clear_ends(padt)
    near(padt)
    take_off(t_land, 0)

    def await_t(d):
        send_t(d).wait_recv()
        take_off(t_land, d)

    each(1, n, await_t)

    def round_aat(r):
        block = acc[r].astype(bf16)
        padt[r + 1] = block
        prop_aat[r] = block

    each(0, nb, round_aat)
    gives.append(pick(2, padt))

    def finish(d):
        ask(d).wait_send()
        send_back(d).wait_send()
        send_page(d).wait_send()
        send_t(d).wait_send()

    each(1, n, finish)
    for j, give in zip((1, 0, 2), gives):
        give.wait_send()
        columns = pl.ds(pl.multiple_of((2 * j + o) * fh, fh), fh)
        remote(
            sel.at[j], feats.at[:, columns], s_pick.at[j], r_pick.at[j], dp=o
        ).wait_recv()


def propagated(pages, band_tiles, off_tiles, off_row, requests, label_page):
    n = lax.axis_size("band")
    tile = band_tiles.shape[-1]
    rows, fh = pages.shape
    nb = rows // tile
    count = label_page.shape[0]
    bf16, f32 = jnp.bfloat16, jnp.float32
    vmem = pl.BlockSpec(memory_space=pltpu.VMEM)
    smem = pl.BlockSpec(memory_space=pltpu.SMEM)
    dma = pltpu.SemaphoreType.DMA
    blocks = jax.ShapeDtypeStruct((nb, tile, fh), bf16)
    per_band = pltpu.VMEM((n, tile, fh), bf16)
    padded = pltpu.VMEM((nb + 2, tile, fh), bf16)
    prop_a, prop_t, prop_aat, feats = pl.pallas_call(
        functools.partial(propagate_kernel, n),
        out_shape=(blocks, blocks, blocks, jax.ShapeDtypeStruct((count // 2, 6 * fh), bf16)),
        in_specs=[vmem, vmem, vmem, smem, vmem, vmem],
        out_specs=(vmem,) * 4,
        scratch_shapes=[
            pltpu.VMEM((count, rows), bf16),
            per_band, per_band, per_band, per_band, per_band, per_band,
            padded, padded,
            pltpu.VMEM((2, tile, fh), f32),
            pltpu.VMEM((2, tile, fh), f32),
            pltpu.VMEM((nb, tile, fh), f32),
            pltpu.VMEM((nb, tile, fh), f32),
            pltpu.VMEM((n, 1, 128), jnp.int32),
            pltpu.SMEM((n, 1, 128), jnp.int32),
            pltpu.VMEM((3, count // 2, fh), bf16),
            dma((1,)),
            *([dma((n,))] * 8), dma((6,)), dma((6,)), dma((3,)), dma((3,)),
        ],
        compiler_params=pltpu.CompilerParams(
            collective_id=1, has_side_effects=True, vmem_limit_bytes=56 * 2**20
        ),
        name="propagate",
    )(
        pages.reshape(nb, tile, fh),
        band_tiles,
        off_tiles,
        off_row,
        jnp.broadcast_to(requests[:, None, None], (n, 1, 128)),
        label_page[:, None],
    )
    return prop_a.reshape(rows, fh), prop_t.reshape(rows, fh), prop_aat.reshape(rows, fh), feats


def per_device(
    pages, band_tiles, off_tiles, off_row, requests, label_page, labels, w_first, w_second
):
    prop_a, prop_t, prop_aat, features = propagated(
        pages, band_tiles, off_tiles, off_row, requests, label_page
    )
    pre_act = jnp.dot(features, w_first, preferred_element_type=jnp.float32)
    sigma = jax.nn.sigmoid(pre_act)
    hidden = (pre_act * sigma).astype(jnp.bfloat16)
    logits = jnp.dot(hidden, w_second, preferred_element_type=jnp.float32)
    probabilities = jax.nn.softmax(logits, axis=-1)
    label_hot = (labels[:, None] == jnp.arange(w_second.shape[1], dtype=jnp.int32)[None, :]).astype(
        jnp.float32
    )
    errors = ((probabilities - label_hot) / label_page.shape[0]).astype(jnp.bfloat16)
    grad_second = jnp.dot(hidden.T, errors, preferred_element_type=jnp.float32)
    slope = sigma * (1.0 + pre_act * (1.0 - sigma))
    back_signal = (jnp.dot(errors, w_second.T, preferred_element_type=jnp.float32) * slope).astype(
        jnp.bfloat16
    )
    grad_first = jnp.dot(features.T, back_signal, preferred_element_type=jnp.float32)
    summed_first, summed_second = summed_gradients(grad_first, grad_second)
    return (
        prop_a,
        prop_t,
        prop_aat,
        summed_first,
        summed_second,
    )


def solution(mesh):
    placed = (
        P("band", "dp"),
        P("band", None, None, None),
        P("band", None, None),
        P("band"),
        P("band"),
        P("band"),
        P(("band", "dp")),
        P(),
        P(),
    )
    return jax.shard_map(
        per_device,
        mesh=mesh,
        in_specs=placed,
        out_specs=(P("band", "dp"), P("band", "dp"), P("band", "dp"), P(), P()),
        check_vma=False,
    )
```

```python
import functools

import jax
import jax.numpy as jnp
from jax import lax
from jax.experimental import pallas as pl
from jax.experimental.pallas import tpu as pltpu
from jax.sharding import PartitionSpec as P


MESH = pl.DeviceIdType.MESH


def greet_all(n):
    b, other = lax.axis_index("band"), 1 - lax.axis_index("dp")
    barrier = pltpu.get_barrier_semaphore()
    pl.semaphore_signal(barrier, inc=1, device_id={"dp": other}, device_id_type=MESH)

    def greet(d, _):
        pl.semaphore_signal(
            barrier, inc=1, device_id={"band": lax.rem(b + d, n)}, device_id_type=MESH
        )
        return 0

    lax.fori_loop(1, n, greet, 0)
    pl.semaphore_wait(barrier, n)


def remote(src, dst, send_sem, recv_sem, **where):
    return pltpu.make_async_remote_copy(
        src_ref=src, dst_ref=dst, send_sem=send_sem, recv_sem=recv_sem,
        device_id=where, device_id_type=MESH,
    )


def each(start, stop, body):
    def step(d, _):
        body(d)
        return 0

    lax.fori_loop(start, stop, step, 0)


def reduce_kernel(
    g, depth, pieces, g1, g2, out, recv1, recv2, cur, land1, land2, land3,
    s_core, r_core, s_one, r_one, s_two, r_two, s_z, r_z,
    s_gz, r_gz, s_g2, r_g2, s_g1, r_g1, s_fw, r_fw,
):
    n = g * g * depth
    b, h = lax.axis_index("band"), lax.axis_index("dp")
    o = 1 - h
    x, y, z = lax.rem(b, g), lax.rem(lax.div(b, g), g), lax.div(b, g * g)
    c1, c2 = x + h * (y - x), y + h * (x - y)
    stride1, stride2 = 1 + h * (g - 1), g - h * (g - 1)
    top, hid = recv1.shape
    low, classes = recv2.shape
    half = out.shape[1]
    quarter = half - top
    rows1 = half // g
    rows2 = rows1 // g
    width = hid // pieces
    thin = width // depth
    low_step = low // pieces
    base1 = c1 * rows1
    base2 = base1 + c2 * rows2
    chunk = 32

    def down(start, size):
        return pl.ds(pl.multiple_of(start, chunk), size)

    def across(start, size):
        return pl.ds(pl.multiple_of(start, 128), size)

    def member1(d):
        m = lax.rem(c1 + d, g)
        return m, b + (m - c1) * stride1

    def member2(d):
        m = lax.rem(c2 + d, g)
        return m, b + (m - c2) * stride2

    def member_z(d):
        m = lax.rem(z + d, depth)
        return m, b + (m - z) * (g * g)

    def core_copies(p):
        w, r = pl.ds(p * width, width), pl.ds(p * low_step, low_step)
        return (
            remote(g1.at[o, :, w], recv1.at[:, w], s_core.at[p, 0], r_core.at[p, 0], dp=o),
            remote(g2.at[o, r], recv2.at[r], s_core.at[p, 1], r_core.at[p, 1], dp=o),
        )

    def one(p, d):
        m, t = member1(d)
        src = cur.at[down(m * rows1, rows1), pl.ds(p * width, width)]
        return remote(src, land1.at[p, d - 1], s_one.at[p, d - 1], r_one.at[p, d - 1], band=t)

    def two(p, d):
        m, t = member2(d)
        src = cur.at[down(base1 + m * rows2, rows2), pl.ds(p * width, width)]
        return remote(src, land2.at[p, d - 1], s_two.at[p, d - 1], r_two.at[p, d - 1], band=t)

    def along_z(p, d):
        m, t = member_z(d)
        src = cur.at[down(base2, rows2), across(p * width + m * thin, thin)]
        return remote(src, land3.at[p, d - 1], s_z.at[p, d - 1], r_z.at[p, d - 1], band=t)

    def back_z(p, d, taking=False):
        m, t = member_z(d)
        owner = lax.rem(z + depth - d, depth) if taking else z
        spot = out.at[h, down(base2, rows2), across(p * width + owner * thin, thin)]
        return remote(spot, spot, s_gz.at[p, d - 1], r_gz.at[p, d - 1], band=t)

    def back2(p, d, taking=False):
        m, t = member2(d)
        owner = lax.rem(c2 + g - d, g) if taking else c2
        spot = out.at[h, down(base1 + owner * rows2, rows2), pl.ds(p * width, width)]
        return remote(spot, spot, s_g2.at[p, d - 1], r_g2.at[p, d - 1], band=t)

    def back1(p, d, taking=False):
        m, t = member1(d)
        owner = lax.rem(c1 + g - d, g) if taking else c1
        spot = out.at[h, down(owner * rows1, rows1), pl.ds(p * width, width)]
        return remote(spot, spot, s_g1.at[p, d - 1], r_g1.at[p, d - 1], band=t)

    def forward(p, core):
        spot = out.at[core, :, pl.ds(p * width, width)]
        return remote(spot, spot, s_fw.at[p], r_fw.at[p], dp=o)

    def begin(p):
        w = pl.ds(p * width, width)
        first, second = core_copies(p)
        first.wait_recv()

        def add_top(i):
            rows = down(i * chunk, chunk)
            cur[rows, w] = g1[h, rows, w] + recv1[rows, w]

        each(0, top // chunk, add_top)
        second.wait_recv()

        def add_low(i):
            for j in range(low_step // quarter):
                rows = down(p * low_step + j * quarter + i * chunk, chunk)
                place = pl.ds(p * width + j * classes, classes)
                cur[down(top + i * chunk, chunk), place] = g2[h, rows] + recv2[rows]

        each(0, quarter // chunk, add_low)
        for d in range(1, g):
            one(p, d).start()

    def gather_in(copies, p, base, rows, land, w):
        for copy in copies:
            copy.wait_recv()

        def add(i):
            spot = down(base + i * chunk, chunk)
            total = cur[spot, w]
            for m in range(len(copies)):
                total += land[p, m, down(i * chunk, chunk)]
            cur[spot, w] = total

        if copies:
            each(0, rows // chunk, add)

    def after_one(p):
        gather_in([one(p, d) for d in range(1, g)], p, base1, rows1, land1, pl.ds(p * width, width))
        for d in range(1, g):
            two(p, d).start()

    def after_two(p):
        gather_in([two(p, d) for d in range(1, g)], p, base2, rows2, land2, pl.ds(p * width, width))
        for d in range(1, depth):
            along_z(p, d).start()

    def after_z(p):
        w = across(p * width + z * thin, thin)
        gather_in([along_z(p, d) for d in range(1, depth)], p, base2, rows2, land3, w)

        def settle(i):
            rows = down(base2 + i * chunk, chunk)
            out[h, rows, w] = cur[rows, w].astype(jnp.bfloat16)

        each(0, rows2 // chunk, settle)
        for d in range(1, depth):
            back_z(p, d).start()

    def after_back_z(p):
        for d in range(1, depth):
            back_z(p, d, True).wait_recv()
        for d in range(1, g):
            back2(p, d).start()

    def after_back2(p):
        for d in range(1, g):
            back2(p, d, True).wait_recv()
        for d in range(1, g):
            back1(p, d).start()

    def after_back1(p):
        for d in range(1, g):
            back1(p, d, True).wait_recv()
        forward(p, h).start()

    greet_all(n)
    for p in range(pieces):
        for copy in core_copies(p):
            copy.start()
    stages = (begin, after_one, after_two, after_z, after_back_z, after_back2, after_back1)
    for t in range(len(stages) + pieces - 1):
        for p in reversed(range(pieces)):
            if 0 <= t - p < len(stages):
                stages[t - p](p)
    for p in range(pieces):
        for copy in core_copies(p):
            copy.wait_send()
        for d in range(1, g):
            for copy in (one(p, d), two(p, d), back2(p, d), back1(p, d)):
                copy.wait_send()
        for d in range(1, depth):
            along_z(p, d).wait_send()
            back_z(p, d).wait_send()
        forward(p, h).wait_send()
        forward(p, o).wait_recv()


def summed_gradients(grad_first, grad_second):
    n = lax.axis_size("band")
    g = max(1, round((n / 2) ** (1 / 3)))
    if n % (g * g):
        g = 1
    depth = n // (g * g)
    in_f, hid = grad_first.shape
    classes = grad_second.shape[1]
    top, low = in_f // 2, hid // 2
    half = (grad_first.size + grad_second.size) // (2 * hid)
    pieces = max(1, hid // (128 * depth))
    width = hid // pieces
    f32 = jnp.float32
    vmem = pl.BlockSpec(memory_space=pltpu.VMEM)
    dma = pltpu.SemaphoreType.DMA
    side, deep = max(1, g - 1), max(1, depth - 1)
    near, far = dma((pieces, side)), dma((pieces, deep))
    packed = pl.pallas_call(
        functools.partial(reduce_kernel, g, depth, pieces),
        out_shape=jax.ShapeDtypeStruct((2, half, hid), jnp.bfloat16),
        in_specs=[vmem] * 2,
        out_specs=vmem,
        scratch_shapes=[
            pltpu.VMEM((top, hid), f32),
            pltpu.VMEM((low, classes), f32),
            pltpu.VMEM((half, hid), f32),
            pltpu.VMEM((pieces, side, half // g, width), f32),
            pltpu.VMEM((pieces, side, half // (g * g), width), f32),
            pltpu.VMEM((pieces, deep, half // (g * g), width // depth), f32),
            dma((pieces, 2)), dma((pieces, 2)),
            near, near, near, near, far, far, far, far, near, near, near, near,
            dma((pieces,)), dma((pieces,)),
        ],
        compiler_params=pltpu.CompilerParams(
            collective_id=0, has_side_effects=True, vmem_limit_bytes=20 * 2**20
        ),
        name="grad_sum",
    )(grad_first.reshape(2, top, hid), grad_second.reshape(2, low, classes))
    parts = hid // classes
    rest = packed[:, top:].reshape(2, half - top, parts, classes)
    return (
        packed[:, :top].reshape(in_f, hid),
        rest.transpose(0, 2, 1, 3).reshape(hid, classes),
    )


def propagate_kernel(
    n, pages, tiles, offs, off_row, req, label, prop_a, prop_t, prop_aat, feats,
    hot, back_send, back_land, page_send, page_land, t_send, t_land, pad, padt,
    rim_send, rim_land, inner, acc, req_out, req_land, served, sel, local_sem,
    s_req, r_req, s_back, r_back, s_page, r_page, s_t, r_t, s_edge, r_edge, s_pick, r_pick,
):
    b, h = lax.axis_index("band"), lax.axis_index("dp")
    o = 1 - h
    nb, tile, fh = pages.shape
    left, right = lax.rem(b + n - 1, n), lax.rem(b + 1, n)
    half = feats.shape[0]
    f32, bf16 = jnp.float32, jnp.bfloat16

    def ahead(d):
        return lax.rem(b + d, n)

    def behind(d):
        return lax.rem(b + n - d, n)

    def tdot(x, y):
        return lax.dot_general(x, y, (((0,), (0,)), ((), ())), preferred_element_type=f32)

    def dot(x, y):
        return jnp.dot(x, y, preferred_element_type=f32)

    barrier = pltpu.get_barrier_semaphore()
    pl.semaphore_signal(barrier, inc=1, device_id={"dp": o}, device_id_type=MESH)
    each(
        1,
        n,
        lambda d: pl.semaphore_signal(
            barrier, inc=1, device_id={"band": ahead(d)}, device_id_type=MESH
        ),
    )
    chunk = label.shape[2]
    lane = lax.broadcasted_iota(jnp.int32, (chunk, chunk), 1)

    def build_hot(i):
        rows = pl.ds(pl.multiple_of(i * chunk, chunk), chunk)
        wanted = jnp.broadcast_to(label[i], (chunk, chunk)).T
        for c in range(nb * tile // chunk):
            hot[rows, c * chunk : (c + 1) * chunk] = jnp.where(
                wanted == lane + c * chunk, 1.0, 0.0
            ).astype(bf16)

    def build_req(t):
        req_out[t] = jnp.full((1, 128), req[t], jnp.int32)

    each(0, n, build_req)
    each(0, hot.shape[0] // chunk, build_hot)
    rim_send[0] = tdot(tiles[0, 0], pages[0])
    rim_send[1] = tdot(tiles[nb - 1, 2], pages[nb - 1])
    pl.semaphore_wait(barrier, n)

    def ask(d):
        t = ahead(d)
        return remote(req_out.at[t], req_land.at[d], s_req.at[d], r_req.at[d], band=t)

    def send_back(d):
        return remote(back_send.at[d], back_land.at[d], s_back.at[d], r_back.at[d], band=ahead(d))

    def send_page(d):
        return remote(page_send.at[d], page_land.at[d], s_page.at[d], r_page.at[d], band=behind(d))

    def send_t(d):
        return remote(t_send.at[d], t_land.at[d], s_t.at[d], r_t.at[d], band=behind(d))

    def edges(source, field, i):
        first, last = source
        return (
            remote(first, field.at[nb + 1], s_edge.at[i], r_edge.at[i], band=left),
            remote(last, field.at[0], s_edge.at[i + 1], r_edge.at[i + 1], band=right),
        )

    each(1, n, lambda d: ask(d).start())
    rims = (
        remote(rim_send.at[0], rim_land.at[0], s_edge.at[2], r_edge.at[2], band=left),
        remote(rim_send.at[1], rim_land.at[1], s_edge.at[3], r_edge.at[3], band=right),
    )
    page_edges = edges((pages.at[0], pages.at[nb - 1]), pad, 0)
    for copy in rims + page_edges:
        copy.start()

    def back_term(d):
        k = ahead(d)
        return tdot(offs[k], pages[off_row[k]]).astype(bf16)

    def make_back(d):
        back_send[d] = back_term(d)
        send_back(d).start()

    each(1, n, make_back)
    back_land[0] = back_term(0)
    req_land[0] = req_out[b]
    each(1, n, lambda d: ask(d).wait_recv())
    to_scalar = pltpu.make_async_copy(req_land, served, local_sem.at[0])
    to_scalar.start()
    to_scalar.wait()

    def make_page(d):
        page_send[d] = pages[served[d, 0, 0]]
        send_page(d).start()

    each(1, n, make_page)
    page_land[0] = pages[served[0, 0, 0]]

    inner[0] = tdot(tiles[0, 1], pages[0]) + tdot(tiles[1, 0], pages[1])
    inner[nb - 1] = tdot(tiles[nb - 1, 1], pages[nb - 1]) + tdot(tiles[nb - 2, 2], pages[nb - 2])

    def adjoint(m):
        inner[m] = (
            tdot(tiles[m - 1, 2], pages[m - 1])
            + tdot(tiles[m, 1], pages[m])
            + tdot(tiles[m + 1, 0], pages[m + 1])
        )

    each(1, nb - 1, adjoint)
    for copy in rims:
        copy.wait()
    inner[nb - 1] += jnp.where(b < n - 1, 1.0, 0.0) * rim_land[0]
    inner[0] += jnp.where(b > 0, 1.0, 0.0) * rim_land[1]

    def spread_rows(target, spot, term):
        for r in range(nb):
            target[r] += jnp.where(spot == r, 1.0, 0.0) * term

    def take_back(d):
        spread_rows(inner, served[d, 0, 0], back_land[d].astype(f32))

    take_back(0)

    def await_back(d):
        send_back(d).wait_recv()
        take_back(d)

    each(1, n, await_back)

    def round_t(r):
        block = inner[r].astype(bf16)
        padt[r + 1] = block
        prop_t[r] = block

    each(0, nb, round_t)
    t_edges = edges((padt.at[1], padt.at[nb]), padt, 4)
    for copy in t_edges:
        copy.start()

    def make_t(d):
        t_send[d] = prop_t[served[d, 0, 0]]
        send_t(d).start()

    each(1, n, make_t)
    t_land[0] = prop_t[served[0, 0, 0]]

    def copy_pages(r):
        pad[r + 1] = pages[r]

    each(0, nb, copy_pages)

    def clear_ends(field):
        @pl.when(b == 0)
        def _():
            field[0] = jnp.zeros((tile, fh), bf16)

        @pl.when(b == n - 1)
        def _():
            field[nb + 1] = jnp.zeros((tile, fh), bf16)

    def near(field):
        def row(r):
            weights = jnp.concatenate([tiles[r, 0], tiles[r, 1], tiles[r, 2]], axis=1)
            window = jnp.concatenate([field[r], field[r + 1], field[r + 2]], axis=0)
            acc[r] = dot(weights, window)

        each(0, nb, row)

    def take_off(land, d):
        k = ahead(d)
        spread_rows(acc, off_row[k], dot(offs[k], land[d]))

    def pick(j, field):
        whole = field[1 : nb + 1].reshape(nb * tile, fh)
        step = half // 2

        def rows_of(core, c):
            return pl.ds(pl.multiple_of(core * half + c * step, step), step)

        columns = pl.ds(pl.multiple_of((2 * j + h) * fh, fh), fh)
        for c in range(2):
            sel[j, c * step : (c + 1) * step] = dot(hot[rows_of(o, c)], whole).astype(bf16)
        give = remote(sel.at[j], feats.at[:, columns], s_pick.at[j], r_pick.at[j], dp=o)
        give.start()
        for c in range(2):
            feats[c * step : (c + 1) * step, columns] = dot(hot[rows_of(h, c)], whole).astype(bf16)
        return give

    gives = [pick(1, padt)]
    for copy in page_edges:
        copy.wait()
    clear_ends(pad)
    near(pad)
    take_off(page_land, 0)

    def await_page(d):
        send_page(d).wait_recv()
        take_off(page_land, d)

    each(1, n, await_page)

    def round_a(r):
        block = acc[r].astype(bf16)
        pad[r + 1] = block
        prop_a[r] = block

    each(0, nb, round_a)
    gives.append(pick(0, pad))
    for copy in t_edges:
        copy.wait()
    clear_ends(padt)
    near(padt)
    take_off(t_land, 0)

    def await_t(d):
        send_t(d).wait_recv()
        take_off(t_land, d)

    each(1, n, await_t)

    def round_aat(r):
        block = acc[r].astype(bf16)
        padt[r + 1] = block
        prop_aat[r] = block

    each(0, nb, round_aat)
    gives.append(pick(2, padt))

    def finish(d):
        ask(d).wait_send()
        send_back(d).wait_send()
        send_page(d).wait_send()
        send_t(d).wait_send()

    each(1, n, finish)
    for j, give in zip((1, 0, 2), gives):
        give.wait_send()
        columns = pl.ds(pl.multiple_of((2 * j + o) * fh, fh), fh)
        remote(
            sel.at[j], feats.at[:, columns], s_pick.at[j], r_pick.at[j], dp=o
        ).wait_recv()


def propagated(pages, band_tiles, off_tiles, off_row, requests, label_page):
    n = lax.axis_size("band")
    tile = band_tiles.shape[-1]
    rows, fh = pages.shape
    nb = rows // tile
    count = label_page.shape[0]
    bf16, f32 = jnp.bfloat16, jnp.float32
    vmem = pl.BlockSpec(memory_space=pltpu.VMEM)
    smem = pl.BlockSpec(memory_space=pltpu.SMEM)
    dma = pltpu.SemaphoreType.DMA
    blocks = jax.ShapeDtypeStruct((nb, tile, fh), bf16)
    per_band = pltpu.VMEM((n, tile, fh), bf16)
    padded = pltpu.VMEM((nb + 2, tile, fh), bf16)
    prop_a, prop_t, prop_aat, feats = pl.pallas_call(
        functools.partial(propagate_kernel, n),
        out_shape=(blocks, blocks, blocks, jax.ShapeDtypeStruct((count // 2, 6 * fh), bf16)),
        in_specs=[vmem, vmem, vmem, smem, smem, vmem],
        out_specs=(vmem,) * 4,
        scratch_shapes=[
            pltpu.VMEM((count, rows), bf16),
            per_band, per_band, per_band, per_band, per_band, per_band,
            padded, padded,
            pltpu.VMEM((2, tile, fh), f32),
            pltpu.VMEM((2, tile, fh), f32),
            pltpu.VMEM((nb, tile, fh), f32),
            pltpu.VMEM((nb, tile, fh), f32),
            pltpu.VMEM((n, 1, 128), jnp.int32),
            pltpu.VMEM((n, 1, 128), jnp.int32),
            pltpu.SMEM((n, 1, 128), jnp.int32),
            pltpu.VMEM((3, count // 2, fh), bf16),
            dma((1,)),
            *([dma((n,))] * 8), dma((6,)), dma((6,)), dma((3,)), dma((3,)),
        ],
        compiler_params=pltpu.CompilerParams(
            collective_id=1, has_side_effects=True, vmem_limit_bytes=56 * 2**20
        ),
        name="propagate",
    )(
        pages.reshape(nb, tile, fh),
        band_tiles,
        off_tiles,
        off_row,
        requests,
        label_page.reshape(count // 128, 1, 128),
    )
    return prop_a.reshape(rows, fh), prop_t.reshape(rows, fh), prop_aat.reshape(rows, fh), feats


def per_device(
    pages, band_tiles, off_tiles, off_row, requests, label_page, labels, w_first, w_second
):
    prop_a, prop_t, prop_aat, features = propagated(
        pages, band_tiles, off_tiles, off_row, requests, label_page
    )
    pre_act = jnp.dot(features, w_first, preferred_element_type=jnp.float32)
    sigma = jax.nn.sigmoid(pre_act)
    hidden = (pre_act * sigma).astype(jnp.bfloat16)
    logits = jnp.dot(hidden, w_second, preferred_element_type=jnp.float32)
    probabilities = jax.nn.softmax(logits, axis=-1)
    label_hot = (labels[:, None] == jnp.arange(w_second.shape[1], dtype=jnp.int32)[None, :]).astype(
        jnp.float32
    )
    errors = ((probabilities - label_hot) / label_page.shape[0]).astype(jnp.bfloat16)
    grad_second = jnp.dot(hidden.T, errors, preferred_element_type=jnp.float32)
    slope = sigma * (1.0 + pre_act * (1.0 - sigma))
    back_signal = (jnp.dot(errors, w_second.T, preferred_element_type=jnp.float32) * slope).astype(
        jnp.bfloat16
    )
    grad_first = jnp.dot(features.T, back_signal, preferred_element_type=jnp.float32)
    summed_first, summed_second = summed_gradients(grad_first, grad_second)
    return (
        prop_a,
        prop_t,
        prop_aat,
        summed_first,
        summed_second,
    )


def solution(mesh):
    placed = (
        P("band", "dp"),
        P("band", None, None, None),
        P("band", None, None),
        P("band"),
        P("band"),
        P("band"),
        P(("band", "dp")),
        P(),
        P(),
    )
    return jax.shard_map(
        per_device,
        mesh=mesh,
        in_specs=placed,
        out_specs=(P("band", "dp"), P("band", "dp"), P("band", "dp"), P(), P()),
        check_vma=False,
    )
```

```python
import functools

import jax
import jax.numpy as jnp
from jax import lax
from jax.experimental import pallas as pl
from jax.experimental.pallas import tpu as pltpu
from jax.sharding import PartitionSpec as P


MESH = pl.DeviceIdType.MESH


def greet_all(n):
    b, other = lax.axis_index("band"), 1 - lax.axis_index("dp")
    barrier = pltpu.get_barrier_semaphore()
    pl.semaphore_signal(barrier, inc=1, device_id={"dp": other}, device_id_type=MESH)

    def greet(d, _):
        pl.semaphore_signal(
            barrier, inc=1, device_id={"band": lax.rem(b + d, n)}, device_id_type=MESH
        )
        return 0

    lax.fori_loop(1, n, greet, 0)
    pl.semaphore_wait(barrier, n)


def remote(src, dst, send_sem, recv_sem, **where):
    return pltpu.make_async_remote_copy(
        src_ref=src, dst_ref=dst, send_sem=send_sem, recv_sem=recv_sem,
        device_id=where, device_id_type=MESH,
    )


def each(start, stop, body):
    def step(d, _):
        body(d)
        return 0

    lax.fori_loop(start, stop, step, 0)


def reduce_kernel(
    g, depth, pieces, feats, w1, w2, label, out, g1, g2, hid_buf, err_buf, back_buf, recv1, recv2, cur, land1, land2, land3,
    s_core, r_core, s_one, r_one, s_two, r_two, s_z, r_z,
    s_gz, r_gz, s_g2, r_g2, s_g1, r_g1, s_fw, r_fw,
):
    n = g * g * depth
    b, h = lax.axis_index("band"), lax.axis_index("dp")
    o = 1 - h
    x, y, z = lax.rem(b, g), lax.rem(lax.div(b, g), g), lax.div(b, g * g)
    c1, c2 = x + h * (y - x), y + h * (x - y)
    stride1, stride2 = 1 + h * (g - 1), g - h * (g - 1)
    top, hid = recv1.shape
    low, classes = recv2.shape
    half = out.shape[1]
    quarter = half - top
    rows1 = half // g
    rows2 = rows1 // g
    width = hid // pieces
    thin = width // depth
    low_step = low // pieces
    base1 = c1 * rows1
    base2 = base1 + c2 * rows2
    chunk = 32

    def down(start, size):
        return pl.ds(pl.multiple_of(start, chunk), size)

    def across(start, size):
        return pl.ds(pl.multiple_of(start, 128), size)

    def member1(d):
        m = lax.rem(c1 + d, g)
        return m, b + (m - c1) * stride1

    def member2(d):
        m = lax.rem(c2 + d, g)
        return m, b + (m - c2) * stride2

    def member_z(d):
        m = lax.rem(z + d, depth)
        return m, b + (m - z) * (g * g)

    def core_copies(p):
        w, r = pl.ds(p * width, width), pl.ds(p * low_step, low_step)
        return (
            remote(g1.at[o, :, w], recv1.at[:, w], s_core.at[p, 0], r_core.at[p, 0], dp=o),
            remote(g2.at[o, r], recv2.at[r], s_core.at[p, 1], r_core.at[p, 1], dp=o),
        )

    def one(p, d):
        m, t = member1(d)
        src = cur.at[down(m * rows1, rows1), pl.ds(p * width, width)]
        return remote(src, land1.at[p, d - 1], s_one.at[p, d - 1], r_one.at[p, d - 1], band=t)

    def two(p, d):
        m, t = member2(d)
        src = cur.at[down(base1 + m * rows2, rows2), pl.ds(p * width, width)]
        return remote(src, land2.at[p, d - 1], s_two.at[p, d - 1], r_two.at[p, d - 1], band=t)

    def along_z(p, d):
        m, t = member_z(d)
        src = cur.at[down(base2, rows2), across(p * width + m * thin, thin)]
        return remote(src, land3.at[p, d - 1], s_z.at[p, d - 1], r_z.at[p, d - 1], band=t)

    def back_z(p, d, taking=False):
        m, t = member_z(d)
        owner = lax.rem(z + depth - d, depth) if taking else z
        spot = out.at[h, down(base2, rows2), across(p * width + owner * thin, thin)]
        return remote(spot, spot, s_gz.at[p, d - 1], r_gz.at[p, d - 1], band=t)

    def back2(p, d, taking=False):
        m, t = member2(d)
        owner = lax.rem(c2 + g - d, g) if taking else c2
        spot = out.at[h, down(base1 + owner * rows2, rows2), pl.ds(p * width, width)]
        return remote(spot, spot, s_g2.at[p, d - 1], r_g2.at[p, d - 1], band=t)

    def back1(p, d, taking=False):
        m, t = member1(d)
        owner = lax.rem(c1 + g - d, g) if taking else c1
        spot = out.at[h, down(owner * rows1, rows1), pl.ds(p * width, width)]
        return remote(spot, spot, s_g1.at[p, d - 1], r_g1.at[p, d - 1], band=t)

    def forward(p, core):
        spot = out.at[core, :, pl.ds(p * width, width)]
        return remote(spot, spot, s_fw.at[p], r_fw.at[p], dp=o)

    def begin(p):
        w = pl.ds(p * width, width)
        first, second = core_copies(p)
        first.wait_recv()

        def add_top(i):
            rows = down(i * chunk, chunk)
            cur[rows, w] = g1[h, rows, w] + recv1[rows, w]

        each(0, top // chunk, add_top)
        second.wait_recv()

        def add_low(i):
            for j in range(low_step // quarter):
                rows = down(p * low_step + j * quarter + i * chunk, chunk)
                place = pl.ds(p * width + j * classes, classes)
                cur[down(top + i * chunk, chunk), place] = g2[h, rows] + recv2[rows]

        each(0, quarter // chunk, add_low)
        for d in range(1, g):
            one(p, d).start()

    def gather_in(copies, p, base, rows, land, w):
        for copy in copies:
            copy.wait_recv()

        def add(i):
            spot = down(base + i * chunk, chunk)
            total = cur[spot, w]
            for m in range(len(copies)):
                total += land[p, m, down(i * chunk, chunk)]
            cur[spot, w] = total

        if copies:
            each(0, rows // chunk, add)

    def after_one(p):
        gather_in([one(p, d) for d in range(1, g)], p, base1, rows1, land1, pl.ds(p * width, width))
        for d in range(1, g):
            two(p, d).start()

    def after_two(p):
        gather_in([two(p, d) for d in range(1, g)], p, base2, rows2, land2, pl.ds(p * width, width))
        for d in range(1, depth):
            along_z(p, d).start()

    def after_z(p):
        w = across(p * width + z * thin, thin)
        gather_in([along_z(p, d) for d in range(1, depth)], p, base2, rows2, land3, w)

        def settle(i):
            rows = down(base2 + i * chunk, chunk)
            out[h, rows, w] = cur[rows, w].astype(jnp.bfloat16)

        each(0, rows2 // chunk, settle)
        for d in range(1, depth):
            back_z(p, d).start()

    def after_back_z(p):
        for d in range(1, depth):
            back_z(p, d, True).wait_recv()
        for d in range(1, g):
            back2(p, d).start()

    def after_back2(p):
        for d in range(1, g):
            back2(p, d, True).wait_recv()
        for d in range(1, g):
            back1(p, d).start()

    def after_back1(p):
        for d in range(1, g):
            back1(p, d, True).wait_recv()
        forward(p, h).start()

    f32, bf16 = jnp.float32, jnp.bfloat16
    span = label.shape[2]
    lane = lax.broadcasted_iota(jnp.int32, (span, span), 1)

    def dot(lhs, rhs, i, j):
        return lax.dot_general(lhs, rhs, (((i,), (j,)), ((), ())), preferred_element_type=f32)

    def step_rows(i):
        rows = pl.ds(pl.multiple_of(i * span, span), span)
        pre = dot(feats[rows], w1[...], 1, 0)
        sigma = jax.nn.sigmoid(pre)
        hidden = (pre * sigma).astype(bf16)
        hid_buf[rows] = hidden
        logits = dot(hidden, w2[...], 1, 0)
        powers = jnp.exp(logits - jnp.max(logits, axis=-1, keepdims=True))
        shares = powers / jnp.sum(powers, axis=-1, keepdims=True)
        wanted = jnp.broadcast_to(label[i], (span, span)).T
        label_hot = jnp.concatenate(
            [jnp.where(wanted == lane + c * span, 1.0, 0.0) for c in range(classes // span)], axis=1
        )
        errors = ((shares - label_hot) / (2 * feats.shape[0])).astype(bf16)
        err_buf[rows] = errors
        slope = sigma * (1.0 + pre * (1.0 - sigma))
        back_buf[rows] = (dot(errors, w2[...], 1, 1) * slope).astype(bf16)

    def gradients(p, core):
        w = pl.ds(p * width, width)

        def first_rows(i):
            source = across(core * top + i * span, span)
            g1[core, down(i * span, span), w] = dot(feats[:, source], back_buf[:, w], 0, 0)

        each(0, top // span, first_rows)

        def second_rows(i):
            source = across(core * low + p * low_step + i * span, span)
            g2[core, down(p * low_step + i * span, span)] = dot(
                hid_buf[:, source], err_buf[...], 0, 0
            )

        each(0, low_step // span, second_rows)

    greet_all(n)
    each(0, feats.shape[0] // span, step_rows)
    for p in range(pieces):
        gradients(p, o)
        for copy in core_copies(p):
            copy.start()
    for p in range(pieces):
        gradients(p, h)
        if p == 0:
            begin(0)
    stages = (begin, after_one, after_two, after_z, after_back_z, after_back2, after_back1)
    for t in range(len(stages) + pieces - 1):
        for p in reversed(range(pieces)):
            if 0 <= t - p < len(stages) and t > 0:
                stages[t - p](p)
    for p in range(pieces):
        for copy in core_copies(p):
            copy.wait_send()
        for d in range(1, g):
            for copy in (one(p, d), two(p, d), back2(p, d), back1(p, d)):
                copy.wait_send()
        for d in range(1, depth):
            along_z(p, d).wait_send()
            back_z(p, d).wait_send()
        forward(p, h).wait_send()
        forward(p, o).wait_recv()


def summed_gradients(features, w_first, w_second, labels):
    n = lax.axis_size("band")
    g = max(1, round((n / 2) ** (1 / 3)))
    if n % (g * g):
        g = 1
    depth = n // (g * g)
    in_f, hid = w_first.shape
    classes = w_second.shape[1]
    count = features.shape[0]
    top, low = in_f // 2, hid // 2
    half = (w_first.size + w_second.size) // (2 * hid)
    pieces = max(1, hid // (128 * depth))
    width = hid // pieces
    f32 = jnp.float32
    vmem = pl.BlockSpec(memory_space=pltpu.VMEM)
    dma = pltpu.SemaphoreType.DMA
    side, deep = max(1, g - 1), max(1, depth - 1)
    near, far = dma((pieces, side)), dma((pieces, deep))
    packed = pl.pallas_call(
        functools.partial(reduce_kernel, g, depth, pieces),
        out_shape=jax.ShapeDtypeStruct((2, half, hid), jnp.bfloat16),
        in_specs=[vmem] * 4,
        out_specs=vmem,
        scratch_shapes=[
            pltpu.VMEM((2, top, hid), f32),
            pltpu.VMEM((2, low, classes), f32),
            pltpu.VMEM((count, hid), jnp.bfloat16),
            pltpu.VMEM((count, classes), jnp.bfloat16),
            pltpu.VMEM((count, hid), jnp.bfloat16),
            pltpu.VMEM((top, hid), f32),
            pltpu.VMEM((low, classes), f32),
            pltpu.VMEM((half, hid), f32),
            pltpu.VMEM((pieces, side, half // g, width), f32),
            pltpu.VMEM((pieces, side, half // (g * g), width), f32),
            pltpu.VMEM((pieces, deep, half // (g * g), width // depth), f32),
            dma((pieces, 2)), dma((pieces, 2)),
            near, near, near, near, far, far, far, far, near, near, near, near,
            dma((pieces,)), dma((pieces,)),
        ],
        compiler_params=pltpu.CompilerParams(
            collective_id=0, has_side_effects=True, vmem_limit_bytes=40 * 2**20
        ),
        name="grad_sum",
    )(features, w_first, w_second, labels.reshape(count // 128, 1, 128))
    parts = hid // classes
    rest = packed[:, top:].reshape(2, half - top, parts, classes)
    return (
        packed[:, :top].reshape(in_f, hid),
        rest.transpose(0, 2, 1, 3).reshape(hid, classes),
    )


def propagate_kernel(
    n, pages, tiles, offs, off_row, req, label, prop_a, prop_t, prop_aat, feats,
    hot, back_send, back_land, page_send, page_land, t_send, t_land, pad, padt,
    rim_send, rim_land, inner, acc, req_out, req_land, served, sel, local_sem,
    s_req, r_req, s_back, r_back, s_page, r_page, s_t, r_t, s_edge, r_edge, s_pick, r_pick,
):
    b, h = lax.axis_index("band"), lax.axis_index("dp")
    o = 1 - h
    nb, tile, fh = pages.shape
    left, right = lax.rem(b + n - 1, n), lax.rem(b + 1, n)
    half = feats.shape[0]
    f32, bf16 = jnp.float32, jnp.bfloat16

    def ahead(d):
        return lax.rem(b + d, n)

    def behind(d):
        return lax.rem(b + n - d, n)

    def tdot(x, y):
        return lax.dot_general(x, y, (((0,), (0,)), ((), ())), preferred_element_type=f32)

    def dot(x, y):
        return jnp.dot(x, y, preferred_element_type=f32)

    barrier = pltpu.get_barrier_semaphore()
    pl.semaphore_signal(barrier, inc=1, device_id={"dp": o}, device_id_type=MESH)
    each(
        1,
        n,
        lambda d: pl.semaphore_signal(
            barrier, inc=1, device_id={"band": ahead(d)}, device_id_type=MESH
        ),
    )
    chunk = label.shape[2]
    lane = lax.broadcasted_iota(jnp.int32, (chunk, chunk), 1)

    def build_hot(i):
        rows = pl.ds(pl.multiple_of(i * chunk, chunk), chunk)
        wanted = jnp.broadcast_to(label[i], (chunk, chunk)).T
        for c in range(nb * tile // chunk):
            hot[rows, c * chunk : (c + 1) * chunk] = jnp.where(
                wanted == lane + c * chunk, 1.0, 0.0
            ).astype(bf16)

    def build_req(t):
        req_out[t] = jnp.full((1, 128), req[t], jnp.int32)

    each(0, n, build_req)
    each(0, hot.shape[0] // chunk, build_hot)
    rim_send[0] = tdot(tiles[0, 0], pages[0])
    rim_send[1] = tdot(tiles[nb - 1, 2], pages[nb - 1])
    pl.semaphore_wait(barrier, n)

    def ask(d):
        t = ahead(d)
        return remote(req_out.at[t], req_land.at[d], s_req.at[d], r_req.at[d], band=t)

    def send_back(d):
        return remote(back_send.at[d], back_land.at[d], s_back.at[d], r_back.at[d], band=ahead(d))

    def send_page(d):
        return remote(page_send.at[d], page_land.at[d], s_page.at[d], r_page.at[d], band=behind(d))

    def send_t(d):
        return remote(t_send.at[d], t_land.at[d], s_t.at[d], r_t.at[d], band=behind(d))

    def edges(source, field, i):
        first, last = source
        return (
            remote(first, field.at[nb + 1], s_edge.at[i], r_edge.at[i], band=left),
            remote(last, field.at[0], s_edge.at[i + 1], r_edge.at[i + 1], band=right),
        )

    each(1, n, lambda d: ask(d).start())
    rims = (
        remote(rim_send.at[0], rim_land.at[0], s_edge.at[2], r_edge.at[2], band=left),
        remote(rim_send.at[1], rim_land.at[1], s_edge.at[3], r_edge.at[3], band=right),
    )
    page_edges = edges((pages.at[0], pages.at[nb - 1]), pad, 0)
    for copy in rims + page_edges:
        copy.start()

    def back_term(d):
        k = ahead(d)
        return tdot(offs[k], pages[off_row[k]]).astype(bf16)

    def make_back(d):
        back_send[d] = back_term(d)
        send_back(d).start()

    each(1, n, make_back)
    back_land[0] = back_term(0)
    req_land[0] = req_out[b]
    each(1, n, lambda d: ask(d).wait_recv())
    to_scalar = pltpu.make_async_copy(req_land, served, local_sem.at[0])
    to_scalar.start()
    to_scalar.wait()

    def make_page(d):
        page_send[d] = pages[served[d, 0, 0]]
        send_page(d).start()

    each(1, n, make_page)
    page_land[0] = pages[served[0, 0, 0]]

    inner[0] = tdot(tiles[0, 1], pages[0]) + tdot(tiles[1, 0], pages[1])
    inner[nb - 1] = tdot(tiles[nb - 1, 1], pages[nb - 1]) + tdot(tiles[nb - 2, 2], pages[nb - 2])

    def adjoint(m):
        inner[m] = (
            tdot(tiles[m - 1, 2], pages[m - 1])
            + tdot(tiles[m, 1], pages[m])
            + tdot(tiles[m + 1, 0], pages[m + 1])
        )

    each(1, nb - 1, adjoint)
    for copy in rims:
        copy.wait()
    inner[nb - 1] += jnp.where(b < n - 1, 1.0, 0.0) * rim_land[0]
    inner[0] += jnp.where(b > 0, 1.0, 0.0) * rim_land[1]

    def spread_rows(target, spot, term):
        for r in range(nb):
            target[r] += jnp.where(spot == r, 1.0, 0.0) * term

    def take_back(d):
        spread_rows(inner, served[d, 0, 0], back_land[d].astype(f32))

    take_back(0)

    def await_back(d):
        send_back(d).wait_recv()
        take_back(d)

    each(1, n, await_back)

    def round_t(r):
        block = inner[r].astype(bf16)
        padt[r + 1] = block
        prop_t[r] = block

    each(0, nb, round_t)
    t_edges = edges((padt.at[1], padt.at[nb]), padt, 4)
    for copy in t_edges:
        copy.start()

    def make_t(d):
        t_send[d] = prop_t[served[d, 0, 0]]
        send_t(d).start()

    each(1, n, make_t)
    t_land[0] = prop_t[served[0, 0, 0]]

    def copy_pages(r):
        pad[r + 1] = pages[r]

    each(0, nb, copy_pages)

    def clear_ends(field):
        @pl.when(b == 0)
        def _():
            field[0] = jnp.zeros((tile, fh), bf16)

        @pl.when(b == n - 1)
        def _():
            field[nb + 1] = jnp.zeros((tile, fh), bf16)

    def near(field):
        def row(r):
            weights = jnp.concatenate([tiles[r, 0], tiles[r, 1], tiles[r, 2]], axis=1)
            window = jnp.concatenate([field[r], field[r + 1], field[r + 2]], axis=0)
            acc[r] = dot(weights, window)

        each(0, nb, row)

    def take_off(land, d):
        k = ahead(d)
        spread_rows(acc, off_row[k], dot(offs[k], land[d]))

    def pick(j, field):
        whole = field[1 : nb + 1].reshape(nb * tile, fh)
        step = half // 2

        def rows_of(core, c):
            return pl.ds(pl.multiple_of(core * half + c * step, step), step)

        columns = pl.ds(pl.multiple_of((2 * j + h) * fh, fh), fh)
        for c in range(2):
            sel[j, c * step : (c + 1) * step] = dot(hot[rows_of(o, c)], whole).astype(bf16)
        give = remote(sel.at[j], feats.at[:, columns], s_pick.at[j], r_pick.at[j], dp=o)
        give.start()
        for c in range(2):
            feats[c * step : (c + 1) * step, columns] = dot(hot[rows_of(h, c)], whole).astype(bf16)
        return give

    gives = [pick(1, padt)]
    for copy in page_edges:
        copy.wait()
    clear_ends(pad)
    near(pad)
    take_off(page_land, 0)

    def await_page(d):
        send_page(d).wait_recv()
        take_off(page_land, d)

    each(1, n, await_page)

    def round_a(r):
        block = acc[r].astype(bf16)
        pad[r + 1] = block
        prop_a[r] = block

    each(0, nb, round_a)
    gives.append(pick(0, pad))
    for copy in t_edges:
        copy.wait()
    clear_ends(padt)
    near(padt)
    take_off(t_land, 0)

    def await_t(d):
        send_t(d).wait_recv()
        take_off(t_land, d)

    each(1, n, await_t)

    def round_aat(r):
        block = acc[r].astype(bf16)
        padt[r + 1] = block
        prop_aat[r] = block

    each(0, nb, round_aat)
    gives.append(pick(2, padt))

    def finish(d):
        ask(d).wait_send()
        send_back(d).wait_send()
        send_page(d).wait_send()
        send_t(d).wait_send()

    each(1, n, finish)
    for j, give in zip((1, 0, 2), gives):
        give.wait_send()
        columns = pl.ds(pl.multiple_of((2 * j + o) * fh, fh), fh)
        remote(
            sel.at[j], feats.at[:, columns], s_pick.at[j], r_pick.at[j], dp=o
        ).wait_recv()


def propagated(pages, band_tiles, off_tiles, off_row, requests, label_page):
    n = lax.axis_size("band")
    tile = band_tiles.shape[-1]
    rows, fh = pages.shape
    nb = rows // tile
    count = label_page.shape[0]
    bf16, f32 = jnp.bfloat16, jnp.float32
    vmem = pl.BlockSpec(memory_space=pltpu.VMEM)
    smem = pl.BlockSpec(memory_space=pltpu.SMEM)
    dma = pltpu.SemaphoreType.DMA
    blocks = jax.ShapeDtypeStruct((nb, tile, fh), bf16)
    per_band = pltpu.VMEM((n, tile, fh), bf16)
    padded = pltpu.VMEM((nb + 2, tile, fh), bf16)
    prop_a, prop_t, prop_aat, feats = pl.pallas_call(
        functools.partial(propagate_kernel, n),
        out_shape=(blocks, blocks, blocks, jax.ShapeDtypeStruct((count // 2, 6 * fh), bf16)),
        in_specs=[vmem, vmem, vmem, smem, smem, vmem],
        out_specs=(vmem,) * 4,
        scratch_shapes=[
            pltpu.VMEM((count, rows), bf16),
            per_band, per_band, per_band, per_band, per_band, per_band,
            padded, padded,
            pltpu.VMEM((2, tile, fh), f32),
            pltpu.VMEM((2, tile, fh), f32),
            pltpu.VMEM((nb, tile, fh), f32),
            pltpu.VMEM((nb, tile, fh), f32),
            pltpu.VMEM((n, 1, 128), jnp.int32),
            pltpu.VMEM((n, 1, 128), jnp.int32),
            pltpu.SMEM((n, 1, 128), jnp.int32),
            pltpu.VMEM((3, count // 2, fh), bf16),
            dma((1,)),
            *([dma((n,))] * 8), dma((6,)), dma((6,)), dma((3,)), dma((3,)),
        ],
        compiler_params=pltpu.CompilerParams(
            collective_id=1, has_side_effects=True, vmem_limit_bytes=56 * 2**20
        ),
        name="propagate",
    )(
        pages.reshape(nb, tile, fh),
        band_tiles,
        off_tiles,
        off_row,
        requests,
        label_page.reshape(count // 128, 1, 128),
    )
    return prop_a.reshape(rows, fh), prop_t.reshape(rows, fh), prop_aat.reshape(rows, fh), feats


def per_device(
    pages, band_tiles, off_tiles, off_row, requests, label_page, labels, w_first, w_second
):
    prop_a, prop_t, prop_aat, features = propagated(
        pages, band_tiles, off_tiles, off_row, requests, label_page
    )
    summed_first, summed_second = summed_gradients(features, w_first, w_second, labels)
    return (
        prop_a,
        prop_t,
        prop_aat,
        summed_first,
        summed_second,
    )


def solution(mesh):
    placed = (
        P("band", "dp"),
        P("band", None, None, None),
        P("band", None, None),
        P("band"),
        P("band"),
        P("band"),
        P(("band", "dp")),
        P(),
        P(),
    )
    return jax.shard_map(
        per_device,
        mesh=mesh,
        in_specs=placed,
        out_specs=(P("band", "dp"), P("band", "dp"), P("band", "dp"), P(), P()),
        check_vma=False,
    )
```
